32 devices in a mesh: phase: 2 (over core), dp: 16 (over z, y, x).
Axes of the slice: x: 2, y: 2, z: 4, core: 2. Of those that a mesh axis runs over, the one named last changes fastest.
Arguments:
- token_vectors: bfloat16 [2, 2, 4096, 1024], P('phase', None, 'dp'), may hold values from -6 to 6
- generation_result_adjoint: bfloat16 [2, 4096, 1024], P(None, 'dp'), may hold values from -6 to 6
- sequence_labels: int32 [2, 16, 256], P(None, 'dp'), may hold values from 0 to 3, never falling along the last dimension, each value on 1 to 192 neighbouring positions
- inquiry_vectors: bfloat16 [2, 2048, 768], P(None, 'dp'), may hold values from -6 to 6
- inquiry_token_spans: int32 [2, 16, 4], P(None, 'dp'), may hold values from 1 to 64, 128 in all within a row
- document_vectors: float32 [2, 256, 768], P(None, 'dp'), may hold values from -0.3 to 0.3
- document_slots: int32 [2, 64, 5], P(None, 'dp'), may hold values from 0 to 15
- relevance_adjoint: float32 [2, 64, 5], P(None, 'dp'), may hold values from -6 to 6
- softness_scalar: float32 [1], replicated, may hold values from 0.5 to 2
- intrinsic_triple_map: bfloat16 [2, 1024, 3072], P('phase', 'dp'), may hold values from -0.1875 to 0.1875
- intrinsic_probe_content_offset: bfloat16 [2, 2048], P('phase', 'dp'), may hold values from -0.59765625 to 0.59765625
- intrinsic_mixing_result_map: bfloat16 [2, 1024, 1024], P('phase', 'dp'), may hold values from -0.75 to 0.75
- intrinsic_mixing_result_offset: bfloat16 [2, 1024], P('phase', 'dp'), may hold values from -1.1953125 to 1.1953125
- perceptron_widen_map: bfloat16 [2, 1024, 4096], P('phase', 'dp'), may hold values from -0.1875 to 0.1875
- perceptron_widen_offset: bfloat16 [2, 4096], P('phase', 'dp'), may hold values from -1.1953125 to 1.1953125
- perceptron_narrow_map: bfloat16 [2, 4096, 1024], P('phase', 'dp'), may hold values from -0.125 to 0.125
- perceptron_narrow_offset: bfloat16 [2, 1024], P('phase', 'dp'), may hold values from -1.1953125 to 1.1953125
- standardize_scales: bfloat16 [2, 2, 1024], P('phase', None, 'dp'), may hold values from 0.5 to 1.5
- standardize_shifts: bfloat16 [2, 2, 1024], P('phase', None, 'dp'), may hold values from -1.1953125 to 1.1953125
- encoded_mixing_probe_map: bfloat16 [1024, 1024], P(('phase', 'dp')), may hold values from -0.1875 to 0.1875
- encoded_mixing_probe_offset: bfloat16 [1024], P(('phase', 'dp')), may hold values from -0.59765625 to 0.59765625
- encoded_lookup_content_map: bfloat16 [1024, 2048], P(('phase', 'dp')), may hold values from -0.1875 to 0.1875
- encoded_mixing_content_offset: bfloat16 [1024], P(('phase', 'dp')), may hold values from -0.59765625 to 0.59765625
- encoded_mixing_result_map: bfloat16 [1024, 1024], P(('phase', 'dp')), may hold values from -0.75 to 0.75
- encoded_mixing_result_offset: bfloat16 [1024], P(('phase', 'dp')), may hold values from -1.1953125 to 1.1953125
- encoded_mixing_scale_factor: bfloat16 [1024], P(('phase', 'dp')), may hold values from 0.5 to 1.5
- encoded_mixing_scale_shift: bfloat16 [1024], P(('phase', 'dp')), may hold values from -1.1953125 to 1.1953125
- retriever_triple_map: bfloat16 [768, 2304], P(('phase', 'dp')), may hold values from -0.21875 to 0.21875
- retriever_probe_content_offset: bfloat16 [1536], P(('phase', 'dp')), may hold values from -0.59765625 to 0.59765625
- retriever_mixing_result_map: bfloat16 [768, 768], P(('phase', 'dp')), may hold values from -0.875 to 0.875
- retriever_mixing_result_offset: bfloat16 [768], P(('phase', 'dp')), may hold values from -1.1953125 to 1.1953125
- retriever_widen_map: bfloat16 [768, 3072], P(('phase', 'dp')), may hold values from -0.21875 to 0.21875
- retriever_widen_offset: bfloat16 [3072], P(('phase', 'dp')), may hold values from -1.1953125 to 1.1953125
- retriever_narrow_map: bfloat16 [3072, 768], P(('phase', 'dp')), may hold values from -0.15625 to 0.15625
- retriever_narrow_offset: bfloat16 [768], P(('phase', 'dp')), may hold values from -1.1953125 to 1.1953125
- retriever_standardize_scales: bfloat16 [2, 768], P(None, ('phase', 'dp')), may hold values from 0.5 to 1.5
- retriever_standardize_shifts: bfloat16 [2, 768], P(None, ('phase', 'dp')), may hold values from -1.1953125 to 1.1953125
Outputs:
- layer_out: bfloat16 [2, 2, 4096, 1024], P('phase', None, 'dp')
- input_grad: float32 [2, 2, 4096, 1024], P('phase', None, 'dp')
- scores: float32 [2, 64, 5], P('phase', 'dp')
- question_grad: float32 [2, 2048, 768], P('phase', 'dp')
- temperature_grad: float32 [1], replicated
- self_qkv_grad: float32 [2, 1024, 3072], P('phase', 'dp')
- self_qv_bias_grad: float32 [2, 2048], P('phase', 'dp')
- self_out_grad: float32 [2, 1024, 1024], P('phase', 'dp')
- self_out_bias_grad: float32 [2, 1024], P('phase', 'dp')
- ffn_in_grad: float32 [2, 1024, 4096], P('phase', 'dp')
- ffn_in_bias_grad: float32 [2, 4096], P('phase', 'dp')
- ffn_out_grad: float32 [2, 4096, 1024], P('phase', 'dp')
- ffn_out_bias_grad: float32 [2, 1024], P('phase', 'dp')
- norm_gain_grad: float32 [2, 2, 1024], P('phase', None, 'dp')
- norm_bias_grad: float32 [2, 2, 1024], P('phase', None, 'dp')
- cross_q_grad: float32 [1024, 1024], P(('phase', 'dp'))
- cross_q_bias_grad: float32 [1024], P(('phase', 'dp'))
- cross_kv_grad: float32 [1024, 2048], P(('phase', 'dp'))
- cross_v_bias_grad: float32 [1024], P(('phase', 'dp'))
- cross_out_grad: float32 [1024, 1024], P(('phase', 'dp'))
- cross_out_bias_grad: float32 [1024], P(('phase', 'dp'))
- cross_norm_gain_grad: float32 [1024], P(('phase', 'dp'))
- cross_norm_bias_grad: float32 [1024], P(('phase', 'dp'))
- query_qkv_grad: float32 [768, 2304], P(('phase', 'dp'))
- query_qv_bias_grad: float32 [1536], P(('phase', 'dp'))
- query_out_grad: float32 [768, 768], P(('phase', 'dp'))
- query_out_bias_grad: float32 [768], P(('phase', 'dp'))
- query_ffn_in_grad: float32 [768, 3072], P(('phase', 'dp'))
- query_ffn_in_bias_grad: float32 [3072], P(('phase', 'dp'))
- query_ffn_out_grad: float32 [3072, 768], P(('phase', 'dp'))
- query_ffn_out_bias_grad: float32 [768], P(('phase', 'dp'))
- query_norm_gain_grad: float32 [2, 768], P(None, ('phase', 'dp'))
- query_norm_bias_grad: float32 [2, 768], P(None, ('phase', 'dp'))
The draws below stay inside these ranges and needn't reach their ends.
Inputs may be any that keep to these rules, and one draw needn't show every extreme that they name: `sequence_labels`: in each block of 256 rows the numbers never fall, each of the 4 sequences has 1 to 192 rows, and one has exactly 192. `inquiry_token_spans`: the 4 lengths of a block sum to 128; the longest is exactly 64. `document_slots`: indices into the 16 passages of the same micro-batch and block.
All inputs are finite; a program needn't handle non-finite values.
Results may differ from the reference program's by a relative error of at most 0.025.
Values may be sent and summed in bfloat16 or wider, within the bound.
No kernel may reach another device: no remote copies, remote signals or barrier semaphores. Data moves between devices by JAX's collectives and lax.ppermute only.
A program may use at most 384 MiB of HBM per device.

```python
import math
import jax
import jax.numpy as jnp
import numpy as np
from jax import lax

D = 1024
HEADS = 16
FF = 4096
DQ = 768
QHEADS = 12
FFQ = 3072
MICRO = 2
ROWS = 256
SEGS = 4
SEG_MOST = 192
QROWS = 128
QSEQ = 4
QMOST = 64
NPASS = 16
KP = 5
BLOCKS = 16
TOKENS = 4096
QTOKENS = 2048
QUESTIONS = 64
PASSAGES = 256
N_DP = 16


def touch_ends(result, own_key, smallest, top_value):
    longest = result.shape.index(max(result.shape))
    spots = []
    for shift in (0, 1):
        where = [jax.random.randint(jax.random.fold_in(own_key, axis), (), 0, length) for axis, length in enumerate(result.shape)]
        where[longest] = (where[longest] + shift) % result.shape[longest]
        spots.append(tuple(where))
    return result.at[spots[0]].set(smallest).at[spots[1]].set(top_value)


def shard_levels(stream_key, shape, pieces, low, high):
    level, own = 1.0, jax.random.fold_in(stream_key, 6)
    for dim, shards_of in pieces:
        steps = jnp.exp(jax.random.uniform(jax.random.fold_in(own, dim), (shards_of,), jnp.float32, low / len(pieces), high / len(pieces)))
        level = level * jnp.repeat(steps, shape[dim] // shards_of).reshape([-1 if axis == dim else 1 for axis in range(len(shape))])
    return level


def profile(count, total, most, slope):
    portions = [(1 << 20) // math.isqrt(grade ** slope) + 1 for grade in range(2, count + 1)]
    spare, given = total - most - (count - 1), [1] * (count - 1)
    while spare > 0:
        free = [i for i in range(count - 1) if given[i] < most]
        mass, budget = sum([portions[i] for i in free]), spare
        for i in free:
            addition = min(most - given[i], max(1, budget * portions[i] // mass), spare)
            given[i] = given[i] + addition
            spare = spare - addition
    return np.array([most] + given)


def ragged_sizes(stream_key, number_of, total, reach, lean):
    if number_of == 2:
        one = jax.random.randint(stream_key, (), max(1, total - reach), min(reach, total - 1) + 1)
        return jnp.stack([one, total - one])
    sizes = jnp.asarray(profile(number_of, total, reach, lean), jnp.int32)
    pairs = (number_of - 1) // 2
    giver, taker = sizes[1:1 + 2 * pairs:2], sizes[2:2 + 2 * pairs:2]
    slack = jnp.minimum(giver - 1, reach - taker)
    passed = jax.random.randint(jax.random.fold_in(stream_key, 1), (pairs,), 0, 1 << 20) % (slack + 1)
    sizes = sizes.at[1:1 + 2 * pairs:2].set(giver - passed).at[2:2 + 2 * pairs:2].set(taker + passed)
    return sizes[jax.random.permutation(jax.random.fold_in(stream_key, 2), number_of)]


def bell_draw(stream_key, extent, scale, limit, cuts=(), kind=jnp.bfloat16):
    result = scale * jax.random.normal(stream_key, extent, jnp.float32)
    if cuts:
        result = result * shard_levels(stream_key, extent, cuts, -0.22, 0.18)
    return jnp.clip(result, -limit, limit).astype(kind)


def setup_inputs(seed: int = 0) -> dict:
    splits = jax.random.split(jax.random.key(seed), 38)
    token_vectors = bell_draw(splits[0], (2, MICRO, TOKENS, D), 1.0, 6.0, ((0, 2), (2, 16)))
    generation_result_adjoint = bell_draw(splits[1], (MICRO, TOKENS, D), 1.0, 6.0, ((1, 16),))
    sequence_labels = jax.vmap(lambda own: jnp.searchsorted(jnp.cumsum(ragged_sizes(own, SEGS, ROWS, SEG_MOST, 2)), jnp.arange(ROWS), side="right"))(jax.random.split(splits[2], MICRO * BLOCKS)).reshape((MICRO, BLOCKS, ROWS)).astype(jnp.int32)
    inquiry_vectors = bell_draw(splits[3], (MICRO, QTOKENS, DQ), 1.0, 6.0, ((1, 16),))
    inquiry_token_spans = jax.vmap(lambda own: ragged_sizes(own, QSEQ, QROWS, QMOST, 2))(jax.random.split(splits[4], MICRO * BLOCKS)).reshape((MICRO, BLOCKS, QSEQ)).astype(jnp.int32)
    document_vectors = bell_draw(splits[5], (MICRO, PASSAGES, DQ), 0.05, 0.3, ((1, 16),), jnp.float32)
    document_slots = touch_ends(jax.random.randint(splits[6], (MICRO, QUESTIONS, KP), 0, NPASS), jax.random.fold_in(splits[6], 1), 0, NPASS - 1).astype(jnp.int32)
    relevance_adjoint = bell_draw(splits[7], (MICRO, QUESTIONS, KP), 1.0, 6.0, ((1, 16),), jnp.float32)
    softness_scalar = jnp.clip(jnp.exp(jax.random.uniform(splits[8], (1,), jnp.float32, math.log(0.5), math.log(2.0))), 0.5, 2.0)
    intrinsic_triple_map = bell_draw(splits[9], (2, D, 3 * D), D ** -0.5, 0.1875, ((0, 2), (1, 16)))
    intrinsic_probe_content_offset = bell_draw(splits[10], (2, 2 * D), 0.1, 0.59765625, ((0, 2), (1, 16)))
    intrinsic_mixing_result_map = bell_draw(splits[11], (2, D, D), (D // 16) ** -0.5, 0.75, ((0, 2), (1, 16)))
    intrinsic_mixing_result_offset = bell_draw(splits[12], (2, D), 0.2, 1.1953125, ((0, 2), (1, 16)))
    perceptron_widen_map = bell_draw(splits[13], (2, D, FF), D ** -0.5, 0.1875, ((0, 2), (1, 16)))
    perceptron_widen_offset = bell_draw(splits[14], (2, FF), 0.2, 1.1953125, ((0, 2), (1, 16)))
    perceptron_narrow_map = bell_draw(splits[15], (2, FF, D), (FF // 2) ** -0.5, 0.125, ((0, 2), (1, 16)))
    perceptron_narrow_offset = bell_draw(splits[16], (2, D), 0.2, 1.1953125, ((0, 2), (1, 16)))
    standardize_scales = jnp.clip(1.0 + 0.1 * jax.random.normal(splits[17], (2, 2, D), jnp.float32), 0.5, 1.5).astype(jnp.bfloat16)
    standardize_shifts = bell_draw(splits[18], (2, 2, D), 0.2, 1.1953125, ((0, 2), (2, 16)))
    encoded_mixing_probe_map = bell_draw(splits[19], (D, D), D ** -0.5, 0.1875, ((0, 32),))
    encoded_mixing_probe_offset = bell_draw(splits[20], (D,), 0.1, 0.59765625, ((0, 32),))
    encoded_lookup_content_map = bell_draw(splits[21], (D, 2 * D), D ** -0.5, 0.1875, ((0, 32),))
    encoded_mixing_content_offset = bell_draw(splits[22], (D,), 0.1, 0.59765625, ((0, 32),))
    encoded_mixing_result_map = bell_draw(splits[23], (D, D), (D // 16) ** -0.5, 0.75, ((0, 32),))
    encoded_mixing_result_offset = bell_draw(splits[24], (D,), 0.2, 1.1953125, ((0, 32),))
    encoded_mixing_scale_factor = jnp.clip(1.0 + 0.1 * jax.random.normal(splits[25], (D,), jnp.float32), 0.5, 1.5).astype(jnp.bfloat16)
    encoded_mixing_scale_shift = bell_draw(splits[26], (D,), 0.2, 1.1953125, ((0, 32),))
    retriever_triple_map = bell_draw(splits[27], (DQ, 3 * DQ), DQ ** -0.5, 0.21875, ((0, 32),))
    retriever_probe_content_offset = bell_draw(splits[28], (2 * DQ,), 0.1, 0.59765625, ((0, 32),))
    retriever_mixing_result_map = bell_draw(splits[29], (DQ, DQ), (DQ // 16) ** -0.5, 0.875, ((0, 32),))
    retriever_mixing_result_offset = bell_draw(splits[30], (DQ,), 0.2, 1.1953125, ((0, 32),))
    retriever_widen_map = bell_draw(splits[31], (DQ, FFQ), DQ ** -0.5, 0.21875, ((0, 32),))
    retriever_widen_offset = bell_draw(splits[32], (FFQ,), 0.2, 1.1953125, ((0, 32),))
    retriever_narrow_map = bell_draw(splits[33], (FFQ, DQ), (FFQ // 2) ** -0.5, 0.15625, ((0, 32),))
    retriever_narrow_offset = bell_draw(splits[34], (DQ,), 0.2, 1.1953125, ((0, 32),))
    retriever_standardize_scales = jnp.clip(1.0 + 0.1 * jax.random.normal(splits[35], (2, DQ), jnp.float32), 0.5, 1.5).astype(jnp.bfloat16)
    retriever_standardize_shifts = bell_draw(splits[36], (2, DQ), 0.2, 1.1953125, ((1, 32),))
    return dict(token_vectors=token_vectors, generation_result_adjoint=generation_result_adjoint, sequence_labels=sequence_labels, inquiry_vectors=inquiry_vectors, inquiry_token_spans=inquiry_token_spans, document_vectors=document_vectors, document_slots=document_slots, relevance_adjoint=relevance_adjoint, softness_scalar=softness_scalar, intrinsic_triple_map=intrinsic_triple_map, intrinsic_probe_content_offset=intrinsic_probe_content_offset, intrinsic_mixing_result_map=intrinsic_mixing_result_map, intrinsic_mixing_result_offset=intrinsic_mixing_result_offset, perceptron_widen_map=perceptron_widen_map, perceptron_widen_offset=perceptron_widen_offset, perceptron_narrow_map=perceptron_narrow_map, perceptron_narrow_offset=perceptron_narrow_offset, standardize_scales=standardize_scales, standardize_shifts=standardize_shifts, encoded_mixing_probe_map=encoded_mixing_probe_map, encoded_mixing_probe_offset=encoded_mixing_probe_offset, encoded_lookup_content_map=encoded_lookup_content_map, encoded_mixing_content_offset=encoded_mixing_content_offset, encoded_mixing_result_map=encoded_mixing_result_map, encoded_mixing_result_offset=encoded_mixing_result_offset, encoded_mixing_scale_factor=encoded_mixing_scale_factor, encoded_mixing_scale_shift=encoded_mixing_scale_shift, retriever_triple_map=retriever_triple_map, retriever_probe_content_offset=retriever_probe_content_offset, retriever_mixing_result_map=retriever_mixing_result_map, retriever_mixing_result_offset=retriever_mixing_result_offset, retriever_widen_map=retriever_widen_map, retriever_widen_offset=retriever_widen_offset, retriever_narrow_map=retriever_narrow_map, retriever_narrow_offset=retriever_narrow_offset, retriever_standardize_scales=retriever_standardize_scales, retriever_standardize_shifts=retriever_standardize_shifts)


@jax.custom_vjp
def low(v):
    return lax.optimization_barrier(v.astype(jnp.bfloat16)).astype(jnp.float32)

@jax.custom_vjp
def low_back(v):
    return v

def low_keep(v):
    return (low(v), None)

def low_pass(kept, grad):
    return (grad,)

def back_keep(v):
    return (v, None)

def back_low(kept, grad):
    return (low(grad),)
low.defvjp(low_keep, low_pass)
low_back.defvjp(back_keep, back_low)
NEG_FILL = -1e+30
EPS_MODEL = 1e-05
EPS_QUERY = 1e-12

def matmul_high(left, right):
    return jnp.dot(left, right, precision=lax.Precision.HIGHEST, preferred_element_type=jnp.float32)

def norm_apply(stream, gain_row, bias_row, epsilon):
    centred = stream - lax.optimization_barrier(jnp.mean(stream, axis=-1, keepdims=True))
    spread = lax.optimization_barrier(jnp.mean(centred * centred, axis=-1, keepdims=True))
    return centred * lax.rsqrt(spread + epsilon) * gain_row + bias_row

def attend(queries, key_rows, value_rows, allowed, head_count):
    total_rows, features = queries.shape
    head_size = features // head_count
    query_heads = queries.reshape(total_rows, head_count, head_size)
    key_heads = key_rows.reshape(key_rows.shape[0], head_count, head_size)
    value_heads = value_rows.reshape(value_rows.shape[0], head_count, head_size)
    scores = jnp.einsum('qhd,khd->hqk', query_heads, key_heads, precision=lax.Precision.HIGHEST) * head_size ** (-0.5)
    scores = low_back(jnp.where(allowed[None], scores, NEG_FILL))
    chances = low(jax.nn.softmax(scores, axis=-1))
    mixed_rows = jnp.einsum('hqk,khd->qhd', chances, value_heads, precision=lax.Precision.HIGHEST)
    return low(low_back(mixed_rows.reshape(total_rows, features)))

def attn_layer(query_low, source_low, coefficient_nest, allowed, head_count):
    query_weight, pair_weight, query_bias, value_bias, proj_weight, proj_bias = coefficient_nest
    features = query_weight.shape[1]
    queries = low(low_back(matmul_high(query_low, query_weight) + query_bias))
    paired = matmul_high(source_low, pair_weight) + jnp.concatenate([jnp.zeros_like(value_bias), value_bias])
    paired = low(low_back(paired))
    mixed_rows = attend(queries, paired[:, :features], paired[:, features:], allowed, head_count)
    return low_back(matmul_high(mixed_rows, proj_weight) + proj_bias)

def feed_layer(stream_low, coefficient_nest):
    up_weight, up_bias, down_weight, down_bias = coefficient_nest
    hidden = low_back(matmul_high(stream_low, up_weight) + up_bias)
    active = low(jax.nn.gelu(hidden, approximate=False))
    return low_back(matmul_high(active, down_weight) + down_bias)

def split_layer(coefficient_nest):
    joined_proj, joined_bias, proj_weight, proj_bias, feed_up, feed_up_bias, feed_down, feed_down_bias, gain_rows, bias_rows = coefficient_nest
    features = joined_proj.shape[0]
    attn_set = (joined_proj[:, :features], joined_proj[:, features:], joined_bias[:features], joined_bias[features:], proj_weight, proj_bias)
    return (attn_set, (feed_up, feed_up_bias, feed_down, feed_down_bias), gain_rows, bias_rows)

def encoder_layer(stream, coefficient_nest, allowed, head_count, epsilon):
    attn_set, feed_set, gain_rows, bias_rows = split_layer(coefficient_nest)
    stream_low = low(stream)
    middle = norm_apply(stream + attn_layer(stream_low, stream_low, attn_set, allowed, head_count), gain_rows[0], bias_rows[0], epsilon)
    return norm_apply(middle + feed_layer(low(middle), feed_set), gain_rows[1], bias_rows[1], epsilon)

def decoder_layer(stream, memory_low, coefficient_nest, cross_set, self_allowed, cross_allowed):
    attn_set, feed_set, gain_rows, bias_rows = split_layer(coefficient_nest)
    cross_query, cross_query_bias, cross_pair, cross_value_bias, cross_proj, cross_proj_bias, cross_gain, cross_bias = cross_set
    stream_low = low(stream)
    first_out = norm_apply(stream + attn_layer(stream_low, stream_low, attn_set, self_allowed, HEADS), gain_rows[0], bias_rows[0], EPS_MODEL)
    cross_attn = (cross_query, cross_pair, cross_query_bias, cross_value_bias, cross_proj, cross_proj_bias)
    second = norm_apply(first_out + attn_layer(low(first_out), memory_low, cross_attn, cross_allowed, HEADS), cross_gain, cross_bias, EPS_MODEL)
    return norm_apply(second + feed_layer(low(second), feed_set), gain_rows[1], bias_rows[1], EPS_MODEL)

def run_block(learnable_nest, source, target, question, segments, lengths, passage_rows, slot_rows):
    phase_set = learnable_nest[:10]
    cross_set = learnable_nest[10:18]
    query_set = learnable_nest[18:28]
    heat_row = learnable_nest[28]
    positions = jnp.arange(segments.shape[0], dtype=jnp.int32)
    same_segment = segments[:, None] == segments[None, :]
    causal = same_segment & (positions[:, None] >= positions[None, :])
    encoder_set = tuple((component_item[0] for component_item in phase_set))
    decoder_set = tuple((component_item[1] for component_item in phase_set))
    memory = encoder_layer(source, encoder_set, same_segment, HEADS, EPS_MODEL)
    decoded = decoder_layer(target, low(low_back(memory)), decoder_set, cross_set, causal, same_segment)
    run_ends = jnp.cumsum(lengths)
    firsts = run_ends - lengths
    question_pos = jnp.arange(question.shape[0], dtype=jnp.int32)
    question_seg = lax.optimization_barrier(jnp.sum((question_pos[:, None] >= run_ends[None, :]).astype(jnp.int32), axis=1))
    question_mask = question_seg[:, None] == question_seg[None, :]
    vectors = encoder_layer(question, query_set, question_mask, QHEADS, EPS_QUERY)[firsts]
    chosen = passage_rows[slot_rows]
    scores = lax.optimization_barrier(jnp.sum(vectors[:, None, :] * chosen, axis=-1)) / heat_row[0]
    return (memory, decoded, scores)

def reference(token_vectors, generation_result_adjoint, sequence_labels, inquiry_vectors, inquiry_token_spans, document_vectors, document_slots, relevance_adjoint, softness_scalar, intrinsic_triple_map, intrinsic_probe_content_offset, intrinsic_mixing_result_map, intrinsic_mixing_result_offset, perceptron_widen_map, perceptron_widen_offset, perceptron_narrow_map, perceptron_narrow_offset, standardize_scales, standardize_shifts, encoded_mixing_probe_map, encoded_mixing_probe_offset, encoded_lookup_content_map, encoded_mixing_content_offset, encoded_mixing_result_map, encoded_mixing_result_offset, encoded_mixing_scale_factor, encoded_mixing_scale_shift, retriever_triple_map, retriever_probe_content_offset, retriever_mixing_result_map, retriever_mixing_result_offset, retriever_widen_map, retriever_widen_offset, retriever_narrow_map, retriever_narrow_offset, retriever_standardize_scales, retriever_standardize_shifts):
    coefficient_nest = (intrinsic_triple_map, intrinsic_probe_content_offset, intrinsic_mixing_result_map, intrinsic_mixing_result_offset, perceptron_widen_map, perceptron_widen_offset, perceptron_narrow_map, perceptron_narrow_offset, standardize_scales, standardize_shifts, encoded_mixing_probe_map, encoded_mixing_probe_offset, encoded_lookup_content_map, encoded_mixing_content_offset, encoded_mixing_result_map, encoded_mixing_result_offset, encoded_mixing_scale_factor, encoded_mixing_scale_shift, retriever_triple_map, retriever_probe_content_offset, retriever_mixing_result_map, retriever_mixing_result_offset, retriever_widen_map, retriever_widen_offset, retriever_narrow_map, retriever_narrow_offset, retriever_standardize_scales, retriever_standardize_shifts)
    learnable_nest = tuple((component_item.astype(jnp.float32) for component_item in coefficient_nest)) + (softness_scalar.astype(jnp.float32),)
    blocks = MICRO * N_DP
    sources = token_vectors[0].astype(jnp.float32).reshape(blocks, ROWS, D)
    targets = token_vectors[1].astype(jnp.float32).reshape(blocks, ROWS, D)
    asked_rows = inquiry_vectors.astype(jnp.float32).reshape(blocks, QROWS, DQ)
    segments = sequence_labels.reshape(blocks, ROWS)
    lengths = inquiry_token_spans.reshape(blocks, QSEQ)
    passage_rows = document_vectors.astype(jnp.float32).reshape(blocks, NPASS, DQ)
    slot_rows = document_slots.reshape(blocks, QSEQ, KP)

    def forward(param_set, source_set, target_set, asked_set):

        def one_block(block_items):
            return run_block(param_set, *block_items)
        return lax.map(jax.checkpoint(one_block), (source_set, target_set, asked_set, segments, lengths, passage_rows, slot_rows))
    (memory, decoded, scores), pull_back = jax.vjp(forward, learnable_nest, sources, targets, asked_rows)
    cotangents = (jnp.zeros_like(memory), generation_result_adjoint.astype(jnp.float32).reshape(blocks, ROWS, D), relevance_adjoint.astype(jnp.float32).reshape(blocks, QSEQ, KP))
    grad_params, grad_sources, grad_targets, grad_asked = pull_back(cotangents)
    layer_out = jnp.stack([memory.reshape(MICRO, N_DP * ROWS, D), decoded.reshape(MICRO, N_DP * ROWS, D)]).astype(jnp.bfloat16)
    input_grad = jnp.stack([grad_sources.reshape(MICRO, N_DP * ROWS, D), grad_targets.reshape(MICRO, N_DP * ROWS, D)])
    return (layer_out, input_grad, scores.reshape(MICRO, N_DP * QSEQ, KP), grad_asked.reshape(MICRO, N_DP * QROWS, DQ), grad_params[28], grad_params[0], grad_params[1], grad_params[2], grad_params[3], grad_params[4], grad_params[5], grad_params[6], grad_params[7], grad_params[8], grad_params[9], grad_params[10], grad_params[11], grad_params[12], grad_params[13], grad_params[14], grad_params[15], grad_params[16], grad_params[17], grad_params[18], grad_params[19], grad_params[20], grad_params[21], grad_params[22], grad_params[23], grad_params[24], grad_params[25], grad_params[26], grad_params[27])
```

```python
from functools import partial

import jax
import jax.numpy as jnp
from jax import lax
from jax.experimental import pallas as pl
from jax.experimental.pallas import tpu as pltpu
from jax.sharding import PartitionSpec as P

HEADS = 16
QHEADS = 12
NEG_FILL = -1e30
EPS_MODEL = 1e-05
EPS_QUERY = 1e-12
BF = jnp.bfloat16
F32 = jnp.float32


def mm(left, right):
    return jnp.dot(left, right, preferred_element_type=F32)


def mm_lt(left, right):
    return lax.dot_general(left, right, (((0,), (0,)), ((), ())), preferred_element_type=F32)


def mm_rt(left, right):
    return lax.dot_general(left, right, (((1,), (1,)), ((), ())), preferred_element_type=F32)


def colsum(matrix):
    return jnp.sum(matrix.astype(F32), axis=0)


def norm_fwd(stream, gain, bias, eps):
    centred = stream - jnp.mean(stream, axis=-1, keepdims=True)
    rstd = lax.rsqrt(jnp.mean(centred * centred, axis=-1, keepdims=True) + eps)
    hat = centred * rstd
    return hat * gain + bias, (hat, rstd)


def norm_bwd(grad, kept, gain):
    hat, rstd = kept
    scaled = grad * gain
    centre = jnp.mean(scaled, axis=-1, keepdims=True)
    along = jnp.mean(scaled * hat, axis=-1, keepdims=True)
    return rstd * (scaled - centre - hat * along), jnp.sum(grad * hat, axis=0), jnp.sum(grad, axis=0)


def gelu_pair(hidden):
    cdf = 0.5 * (1.0 + lax.erf(hidden * 0.7071067811865476))
    pdf = jnp.exp(-0.5 * hidden * hidden) * 0.3989422804014327
    return (hidden * cdf).astype(BF), (cdf + hidden * pdf).astype(BF)


def allowed_bias(key_ref, query_ref, causal_ref):
    same = key_ref[0] == query_ref[0]
    keys = lax.broadcasted_iota(jnp.int32, same.shape, 0)
    queries = lax.broadcasted_iota(jnp.int32, same.shape, 1)
    seen = jnp.logical_and(same, jnp.logical_or(queries >= keys, causal_ref[0] == 0))
    return jnp.where(seen, 0.0, NEG_FILL).astype(F32)


def attn_fwd_body(
    head_size, q_off, k_off, v_off, causal_ref, key_ref, query_ref, q_ref, k_ref, v_ref, o_ref
):
    bias = allowed_bias(key_ref, query_ref, causal_ref)
    scale = head_size ** (-0.5)
    pairs = o_ref.shape[1] // 128

    def one(pair, carry):
        at = pl.multiple_of(pair * 128, 128)
        q2 = q_ref[:, pl.ds(q_off + at, 128)]
        q2 = (q2.astype(F32) * scale).astype(BF)
        k2 = k_ref[:, pl.ds(k_off + at, 128)]
        v_t = v_ref[:, pl.ds(v_off + at, 128)].T
        lane = lax.broadcasted_iota(jnp.int32, q2.shape, 1) < head_size
        mixed = []
        for mine in (lane, jnp.logical_not(lane)):
            scores = mm_rt(k2, jnp.where(mine, q2, jnp.zeros_like(q2))) + bias
            raised = jnp.exp(scores - jnp.max(scores, axis=0, keepdims=True))
            total = jnp.sum(raised, axis=0, keepdims=True)
            mixed.append(mm(v_t, raised.astype(BF)) * (1.0 / total))
        row = lax.broadcasted_iota(jnp.int32, mixed[0].shape, 0) < head_size
        o_ref[:, pl.ds(at, 128)] = jnp.where(row, mixed[0], mixed[1]).T.astype(BF)
        return carry

    lax.fori_loop(0, pairs, one, 0)


def attn_bwd_body(
    head_size, q_off, k_off, v_off, joint, causal_ref, key_ref, query_ref, q_ref, k_ref, v_ref, g_ref, *outs
):
    bias = allowed_bias(key_ref, query_ref, causal_ref)
    scale = head_size ** (-0.5)
    pairs = g_ref.shape[1] // 128
    dq_ref, dk_ref, dv_ref = (outs[0],) * 3 if joint else (outs[0], outs[1], outs[1])

    def one(pair, carry):
        at = pl.multiple_of(pair * 128, 128)
        q2 = q_ref[:, pl.ds(q_off + at, 128)]
        q2 = (q2.astype(F32) * scale).astype(BF)
        k2 = k_ref[:, pl.ds(k_off + at, 128)]
        v2 = v_ref[:, pl.ds(v_off + at, 128)]
        g2 = g_ref[:, pl.ds(at, 128)]
        k_t = k2.T
        lane = lax.broadcasted_iota(jnp.int32, q2.shape, 1) < head_size
        parts = []
        for mine in (lane, jnp.logical_not(lane)):
            scores = mm_rt(k2, jnp.where(mine, q2, jnp.zeros_like(q2))) + bias
            raised = jnp.exp(scores - jnp.max(scores, axis=0, keepdims=True))
            chances = raised * (1.0 / jnp.sum(raised, axis=0, keepdims=True))
            grad_p = mm_rt(v2, jnp.where(mine, g2, jnp.zeros_like(g2)))
            inner = jnp.sum(chances * grad_p, axis=0, keepdims=True)
            grad_s = (chances * (grad_p - inner)).astype(BF)
            grad_v = mm(chances.astype(BF), g2)
            grad_k = mm(grad_s, q2)
            grad_q_t = mm(k_t, grad_s)
            parts.append((grad_q_t, grad_k, grad_v))
        row = lax.broadcasted_iota(jnp.int32, parts[0][0].shape, 0) < head_size
        grad_q = jnp.where(row, parts[0][0], parts[1][0]).T * scale
        dq_ref[:, pl.ds(q_off + at, 128)] = grad_q.astype(BF)
        dk_ref[:, pl.ds(k_off + at, 128)] = jnp.where(lane, parts[0][1], parts[1][1]).astype(BF)
        dv_ref[:, pl.ds(v_off + at, 128)] = jnp.where(lane, parts[0][2], parts[1][2]).astype(BF)
        return carry

    lax.fori_loop(0, pairs, one, 0)


def attn_specs(rows, arrays):
    specs = [
        pl.BlockSpec(memory_space=pltpu.SMEM),
        pl.BlockSpec((1, rows, 1), lambda m: (m, 0, 0)),
        pl.BlockSpec((1, 1, rows), lambda m: (m, 0, 0)),
    ]
    return specs + [pl.BlockSpec((rows, a.shape[1]), lambda m: (m, 0)) for a in arrays]


def attn_params():
    return pltpu.CompilerParams(dimension_semantics=("arbitrary",), vmem_limit_bytes=48 << 20)


def attn_cost(total, rows, width, products):
    return pl.CostEstimate(
        flops=2 * products * total * rows * width,
        transcendentals=total * rows * HEADS,
        bytes_accessed=total * width * 2 * (4 if products == 2 else 7),
    )


def attend(q, k, v, offsets, width, labels, causal):
    rows = labels.shape[1]
    total = q.shape[0]
    return pl.pallas_call(
        partial(attn_fwd_body, width // HEADS, *offsets),
        grid=(total // rows,),
        in_specs=attn_specs(rows, (q, k, v)),
        out_specs=pl.BlockSpec((rows, width), lambda m: (m, 0)),
        out_shape=jax.ShapeDtypeStruct((total, width), BF),
        compiler_params=attn_params(),
        cost_estimate=attn_cost(total, rows, width, 2),
        name="attend_fwd",
    )(causal, labels[:, :, None], labels[:, None, :], q, k, v)


def attend_back(q, k, v, offsets, width, labels, causal, grad, joint):
    rows = labels.shape[1]
    total = q.shape[0]
    widths = (3 * width,) if joint else (width, 2 * width)
    out = pl.pallas_call(
        partial(attn_bwd_body, width // HEADS, *offsets, joint),
        grid=(total // rows,),
        in_specs=attn_specs(rows, (q, k, v, grad)),
        out_specs=[pl.BlockSpec((rows, w), lambda m: (m, 0)) for w in widths],
        out_shape=[jax.ShapeDtypeStruct((total, w), BF) for w in widths],
        compiler_params=attn_params(),
        cost_estimate=attn_cost(total, rows, width, 5),
        name="attend_bwd",
    )(causal, labels[:, :, None], labels[:, None, :], q, k, v, grad)
    return out[0] if joint else tuple(out)


def heads_of(matrix, count):
    return matrix.reshape(matrix.shape[0], count, matrix.shape[1] // count)


def query_work(
    rows_bf, firsts, ends, chosen, adjoint, heat, sheet, hidden_size, shards, vectors
):
    b_joint, b_out, b_up, b_down, gains, shifts = vectors
    width = rows_bf.shape[1]
    folds = hidden_size // width
    w_joint = sheet[:, : 3 * width]
    w_out = sheet[:, 3 * width : 4 * width]
    w_up = sheet[:, 4 * width : 4 * width + hidden_size]
    downs = [
        sheet[:, 4 * width + hidden_size + i * width : 5 * width + hidden_size + i * width]
        for i in range(folds)
    ]

    def fold(matrix):
        split = matrix.reshape(matrix.shape[0], shards, folds, -1)
        return [split[:, :, i].reshape(matrix.shape[0], width) for i in range(folds)]

    def unfold(parts):
        split = [p.reshape(p.shape[0], shards, 1, -1) for p in parts]
        return jnp.concatenate(split, axis=2).reshape(parts[0].shape[0], -1)

    scale = (width // QHEADS) ** (-0.5)
    positions = jnp.arange(rows_bf.shape[0], dtype=jnp.int32)
    allowed = (positions[None, :] >= firsts[:, None]) & (positions[None, :] < ends[:, None])
    pick = (positions[None, :] == firsts[:, None]).astype(BF)
    head_bf = mm(pick, rows_bf).astype(BF)
    queries = (mm(head_bf, w_joint[:, :width]) + b_joint[:width]).astype(BF)
    paired = mm(rows_bf, w_joint[:, width:])
    keys = paired[:, :width].astype(BF)
    values = (paired[:, width:] + b_joint[width:]).astype(BF)
    qh, kh, vh = heads_of(queries, QHEADS), heads_of(keys, QHEADS), heads_of(values, QHEADS)
    scores = jnp.einsum("qhd,khd->hqk", qh, kh, preferred_element_type=F32) * scale
    scores = jnp.where(allowed[None], scores, NEG_FILL)
    chances = jax.nn.softmax(scores, axis=-1)
    chances_bf = chances.astype(BF)
    mixed = jnp.einsum("hqk,khd->qhd", chances_bf, vh, preferred_element_type=F32)
    mixed = mixed.reshape(queries.shape).astype(BF)
    branch = mm(mixed, w_out) + b_out
    middle, kept_one = norm_fwd(head_bf.astype(F32) + branch, gains[0], shifts[0], EPS_QUERY)
    middle_bf = middle.astype(BF)
    active, slope = gelu_pair(mm(middle_bf, w_up) + b_up)
    folded = fold(active)
    fed = sum(mm(part, down) for part, down in zip(folded, downs))
    found, kept_two = norm_fwd(middle + fed + b_down, gains[1], shifts[1], EPS_QUERY)
    raw = jnp.sum(found[:, None, :] * chosen, axis=-1)
    scored = raw / heat
    grad_heat = -jnp.sum(adjoint * raw) / (heat * heat)
    grad_found = jnp.sum((adjoint / heat)[:, :, None] * chosen, axis=1)
    grad_two, gain_two, shift_two = norm_bwd(grad_found, kept_two, gains[1])
    grad_two_bf = grad_two.astype(BF)
    grad_active = unfold([mm_rt(grad_two_bf, down) for down in downs])
    grad_hidden = (grad_active * slope.astype(F32)).astype(BF)
    grad_middle = grad_two + mm_rt(grad_hidden, w_up)
    grad_one, gain_one, shift_one = norm_bwd(grad_middle, kept_one, gains[0])
    grad_one_bf = grad_one.astype(BF)
    grad_mixed = heads_of(mm_rt(grad_one_bf, w_out).astype(BF), QHEADS)
    grad_values = jnp.einsum("hqk,qhd->khd", chances_bf, grad_mixed, preferred_element_type=F32)
    grad_chances = jnp.einsum("qhd,khd->hqk", grad_mixed, vh, preferred_element_type=F32)
    inner = jnp.sum(chances * grad_chances, axis=-1, keepdims=True)
    grad_scores = (chances * (grad_chances - inner)).astype(BF)
    grad_q = jnp.einsum("hqk,khd->qhd", grad_scores, kh, preferred_element_type=F32) * scale
    grad_k = jnp.einsum("hqk,qhd->khd", grad_scores, qh, preferred_element_type=F32) * scale
    grad_q = grad_q.reshape(queries.shape).astype(BF)
    grad_kv = jnp.concatenate(
        [grad_k.reshape(keys.shape), grad_values.reshape(keys.shape)], axis=1
    ).astype(BF)
    grad_heads = grad_one + mm_rt(grad_q, w_joint[:, :width])
    spread = lax.dot_general(
        pick.astype(F32), grad_heads, (((0,), (0,)), ((), ())),
        precision=lax.Precision.HIGHEST, preferred_element_type=F32,
    )
    grad_rows = mm_rt(grad_kv, w_joint[:, width:]) + spread
    factors = [
        head_bf, grad_q, mixed, grad_one_bf, middle_bf, grad_hidden, active, grad_two_bf,
        queries, grad_mixed.reshape(queries.shape),
    ]
    seen = [
        jnp.einsum("hqk,kd->qhd", p, rows_bf, preferred_element_type=F32)
        for p in (grad_scores, chances_bf)
    ]
    seen = jnp.concatenate(seen, axis=2).astype(BF).reshape(-1, 2 * width)
    flat = jnp.concatenate(factors, axis=1).reshape(seen.shape[0], -1)
    mats = jnp.concatenate([seen, flat], axis=1)
    smalls = (
        jnp.concatenate([colsum(grad_q), colsum(grad_kv[:, width:])]),
        colsum(grad_one_bf),
        colsum(grad_hidden),
        colsum(grad_two_bf),
        jnp.stack([gain_one, gain_two]),
        jnp.stack([shift_one, shift_two]),
    )
    return scored, grad_rows, grad_heat, mats, smalls


class Links:
    def __init__(self):
        self.n = lax.axis_size("dp")
        self.half = self.n // 2
        self.bits = self.half.bit_length() - 1
        self.core = lax.axis_index("phase")
        self.dp = lax.axis_index("dp")
        self.is_enc = self.dp < self.half

    def all_pairs(self, value, pairs):
        return lax.ppermute(value, ("phase", "dp"), pairs)

    def swap(self, value):
        n, h = self.n, self.half
        pairs = []
        for i in range(h):
            pairs += [(i, i), (n + i, i + h), (i + h, n + i), (n + i + h, n + i + h)]
        return self.all_pairs(value, pairs)

    def pull_enc(self, value):
        n, h = self.n, self.half
        pairs = []
        for i in range(h):
            pairs += [(i, i), (i + h, n + i)]
        return self.all_pairs(value, pairs)

    def home_enc(self, value):
        n, h = self.n, self.half
        pairs = []
        for i in range(h):
            pairs += [(i, i), (n + i, i + h)]
        return self.all_pairs(value, pairs)

    def push_dec(self, value):
        n, h = self.n, self.half
        pairs = []
        for i in range(h):
            pairs += [(n + i + h, n + i + h), (n + i, i + h)]
        return self.all_pairs(value, pairs)

    def to_dec(self, value):
        return lax.ppermute(value, "dp", [(i, i + self.half) for i in range(self.half)])

    def to_enc(self, value):
        return lax.ppermute(value, "dp", [(i + self.half, i) for i in range(self.half)])

    def across(self, value):
        h = self.half
        pairs = [(i, i + h) for i in range(h)] + [(i + h, i) for i in range(h)]
        return lax.ppermute(value, "dp", pairs)

    def flip(self, value, who="both"):
        first = self.half if who == "dec" else 0
        last = self.half if who == "enc" else self.n
        pairs = []
        for i in range(first, last):
            pairs += [(i, self.n + i), (self.n + i, i)]
        return self.all_pairs(value, pairs)

    def hop(self, value, bit, who):
        first = self.half if who == "dec" else 0
        last = self.half if who == "enc" else self.n
        return lax.ppermute(value, "dp", [(i, i ^ (1 << bit)) for i in range(first, last)])

    def order(self, turn):
        return [(turn + k) % self.bits for k in range(self.bits)]

    def gather_hop(self, held, turn, step, who="both"):
        return self.hop(held, self.order(turn)[step], who)

    def places(self, turn, lead=1):
        order = self.order(turn)
        mine = self.dp % self.half
        masks = [
            sum(((p >> j) & 1) << order[j] for j in range(self.bits)) for p in range(self.half)
        ]
        own = jnp.stack(
            [jnp.bitwise_xor(mine, m) + r * self.half for m in masks for r in range(lead)]
        ).astype(jnp.int32)
        wide = lead * self.half
        return jnp.concatenate([own + self.core * wide, own + (1 - self.core) * wide])

    def half_of(self, left, core):
        wide = left.shape[1] // 2
        return lax.dynamic_slice_in_dim(left, core * wide, wide, 1)

    def reduce_open(self, left, right):
        return self.flip(mm_lt(self.half_of(left, 1 - self.core), right).astype(BF))

    def reduce_own(self, left, right, got):
        own = mm_lt(self.half_of(left, self.core), right) + got.astype(F32)
        shard = left.shape[1] // self.n
        return own.astype(BF).reshape((2,) * self.bits + (shard, right.shape[1]))

    def reduce_step(self, value, turn, step, who="both", lead=0):
        bit = self.order(turn)[step]
        mine = (self.dp >> bit) & 1
        axis = lead + self.bits - 1 - bit
        send = lax.dynamic_slice_in_dim(value, 1 - mine, 1, axis)
        keep = lax.dynamic_slice_in_dim(value, mine, 1, axis)
        got = self.hop(send, bit, who)
        return (keep.astype(F32) + got.astype(F32)).astype(value.dtype)


def weave_body(quarter, streams, place_ref, *refs):
    count = len(streams)
    at = pl.program_id(0)
    for index in range(4):

        @pl.when(jnp.logical_and(at >= index * quarter, at < (index + 1) * quarter))
        def _(index=index):
            out = 4 * count
            for stream, widths in enumerate(streams):
                low = 0
                for width in widths:
                    refs[out][...] = refs[4 * stream + index][0, :, low : low + width]
                    low += width
                    out += 1


def weave(streams, places, widths):
    quarter = streams[0][0].shape[0]
    total = 4 * quarter

    def source(part, index):
        return pl.BlockSpec(
            (1,) + part.shape[1:],
            lambda g, place: (jnp.clip(g - index * quarter, 0, quarter - 1), 0, 0),
        )

    def target(rows, width, stream):
        return pl.BlockSpec((rows, width), lambda g, place: (place[stream, g], 0))

    shapes = [
        (parts[0].shape[1], w, i)
        for i, (parts, ws) in enumerate(zip(streams, widths))
        for w in ws
    ]
    moved = sum(4 * p.size for parts in streams for p in parts)
    return pl.pallas_call(
        partial(weave_body, quarter, widths),
        grid_spec=pltpu.PrefetchScalarGridSpec(
            num_scalar_prefetch=1,
            grid=(total,),
            in_specs=[source(p, i) for parts in streams for i, p in enumerate(parts)],
            out_specs=[target(*shape) for shape in shapes],
        ),
        out_shape=[jax.ShapeDtypeStruct((total * r, w), BF) for r, w, _ in shapes],
        compiler_params=pltpu.CompilerParams(
            dimension_semantics=("arbitrary",), vmem_limit_bytes=48 << 20
        ),
        cost_estimate=pl.CostEstimate(flops=0, transcendentals=0, bytes_accessed=moved),
        name="weave",
    )(places, *[p for parts in streams for p in parts])


def stage(*values):
    return lax.optimization_barrier(values)


def block_of(values, rows):
    flat = jnp.concatenate([v.reshape(1, -1).astype(BF) for v in values], axis=1)
    return jnp.pad(flat, ((0, 0), (0, rows * 128 - flat.size))).reshape(rows, 128)


def local(
    token_vectors,
    generation_result_adjoint,
    sequence_labels,
    inquiry_vectors,
    inquiry_token_spans,
    document_vectors,
    document_slots,
    relevance_adjoint,
    softness_scalar,
    intrinsic_triple_map,
    intrinsic_probe_content_offset,
    intrinsic_mixing_result_map,
    intrinsic_mixing_result_offset,
    perceptron_widen_map,
    perceptron_widen_offset,
    perceptron_narrow_map,
    perceptron_narrow_offset,
    standardize_scales,
    standardize_shifts,
    encoded_mixing_probe_map,
    encoded_mixing_probe_offset,
    encoded_lookup_content_map,
    encoded_mixing_content_offset,
    encoded_mixing_result_map,
    encoded_mixing_result_offset,
    encoded_mixing_scale_factor,
    encoded_mixing_scale_shift,
    retriever_triple_map,
    retriever_probe_content_offset,
    retriever_mixing_result_map,
    retriever_mixing_result_offset,
    retriever_widen_map,
    retriever_widen_offset,
    retriever_narrow_map,
    retriever_narrow_offset,
    retriever_standardize_scales,
    retriever_standardize_shifts,
):
    links = Links()
    n, half, is_enc, core = links.n, links.half, links.is_enc, links.core
    micro, rows, width = token_vectors.shape[1:]
    total = micro * rows
    joint_w = intrinsic_triple_map.shape[2]
    ff = perceptron_widen_map.shape[2]
    heat = softness_scalar[0]

    role_vecs = (
        intrinsic_probe_content_offset,
        intrinsic_mixing_result_offset,
        perceptron_widen_offset,
        perceptron_narrow_offset,
        standardize_scales,
        standardize_shifts,
    )
    cross_vecs = (
        encoded_mixing_probe_offset,
        encoded_mixing_content_offset,
        encoded_mixing_result_offset,
        encoded_mixing_scale_factor,
        encoded_mixing_scale_shift,
    )
    query_vecs = (
        retriever_probe_content_offset,
        retriever_mixing_result_offset,
        retriever_widen_offset,
        retriever_narrow_offset,
        retriever_standardize_scales,
        retriever_standardize_shifts,
    )
    n_role = sum(v.size for v in role_vecs)
    n_cross = sum(v.size for v in cross_vecs)
    n_query = sum(v.size for v in query_vecs)
    everyone = ("phase", "dp")
    shard_rows = intrinsic_triple_map.shape[1]
    q_width = inquiry_vectors.shape[2]
    q_ff = retriever_widen_map.shape[1]
    q_rows = retriever_triple_map.shape[0]
    q_folds = q_ff // q_width
    cross_rows = encoded_mixing_probe_map.shape[0]

    def vectors_of(table, like):
        at, out = 0, []
        for vec in like:
            lead = vec.shape[-2] if vec.ndim > 1 and vec.shape[-2] > 1 else 1
            piece = table[:, at : at + vec.size].reshape(table.shape[0], lead, -1)
            piece = piece.transpose(1, 0, 2).reshape(lead, -1)
            out.append(piece if lead > 1 else piece[0])
            at += vec.size
        return out

    attn_in = jnp.concatenate(
        [
            intrinsic_triple_map[0],
            intrinsic_mixing_result_map[0],
            block_of(role_vecs + (sequence_labels,), shard_rows),
        ],
        axis=1,
    )
    held = list(
        stage(
            links.swap(attn_in),
            links.swap(perceptron_widen_map[0]),
            links.swap(perceptron_narrow_map[0]),
        )
    )
    labels = held[0][:, joint_w + width :].reshape(1, -1)[:, n_role : n_role + total]
    labels = labels.astype(jnp.int32).reshape(micro, rows)
    held = [v[None] for v in held]
    tokens_in, held = stage(token_vectors[0].reshape(total, width), held)
    stream_bf = links.swap(tokens_in)
    adjoint_own = generation_result_adjoint.reshape(total, width)
    query_in = jnp.concatenate(
        [retriever_triple_map, retriever_mixing_result_map, retriever_widen_map]
        + [retriever_narrow_map[i * q_rows : (i + 1) * q_rows] for i in range(q_folds)]
        + [block_of(query_vecs, q_rows)],
        axis=1,
    )
    cross_in = jnp.concatenate(
        [
            encoded_mixing_probe_map,
            encoded_lookup_content_map,
            encoded_mixing_result_map,
            block_of(cross_vecs, cross_rows),
        ],
        axis=1,
    )
    asked = inquiry_token_spans.shape[2]
    chosen_count = document_slots.shape[2]
    ints = jnp.concatenate(
        [
            inquiry_token_spans.reshape(1, -1).astype(F32),
            document_slots.reshape(1, -1).astype(F32),
            relevance_adjoint.reshape(1, -1),
        ],
        axis=1,
    )
    doc_own = jnp.concatenate(
        [
            document_vectors.reshape(-1, q_width),
            jnp.pad(ints, ((0, 0), (0, q_width - ints.size))),
        ]
    )
    q_own = inquiry_vectors.reshape(-1, q_width)
    last = links.bits - 1
    for step in range(last):
        held = [
            jnp.concatenate([v, links.gather_hop(v, turn, step)], axis=0)
            for turn, v in enumerate(held)
        ]
        if step == 0:
            held, stream_bf, adjoint_own, cross_in, doc_own, q_own = stage(
                held, stream_bf, adjoint_own, cross_in, doc_own, q_own
            )
            cross_full = lax.all_gather(cross_in, everyone, axis=0, tiled=True)
        else:
            (held,) = stage(held)
    recv = [links.gather_hop(v, turn, last) for turn, v in enumerate(held)]
    theirs = [links.flip(v) for v in held]
    adjoint_bf = links.push_dec(adjoint_own)
    doc_packet = links.pull_enc(doc_own)
    q_block_rows = links.pull_enc(q_own)
    recv, theirs, adjoint_bf, query_in, doc_packet, q_block_rows = stage(
        recv, theirs, adjoint_bf, query_in, doc_packet, q_block_rows
    )
    query_full = lax.all_gather(query_in, everyone, axis=0, tiled=True)
    got = [links.flip(v) for v in recv]
    w_joint, w_out, w_small, w_up, w_down = weave(
        list(zip(held, recv, theirs, got)),
        jnp.stack([links.places(turn) for turn in range(3)]),
        ((joint_w, width, 128), (ff,), (width,)),
    )
    mine_small = w_small.reshape(n, -1)[:, :n_role].astype(F32)
    b_joint, b_out, b_up, b_down, gains, shifts = vectors_of(mine_small, role_vecs)

    causal = jnp.where(is_enc, 0, 1).astype(jnp.int32).reshape(1)
    plain = jnp.zeros((1,), jnp.int32)
    stream = stream_bf.astype(F32)
    bias_joint = jnp.concatenate([b_joint[:width], jnp.zeros((width,), F32), b_joint[width:]])
    joint = (mm(stream_bf, w_joint) + bias_joint).astype(BF)
    self_off = (0, width, 2 * width)
    mixed = attend(joint, joint, joint, self_off, width, labels, causal)
    first, kept_one = norm_fwd(stream + mm(mixed, w_out) + b_out, gains[0], shifts[0], EPS_MODEL)
    first_bf = first.astype(BF)

    def feed(stream_one, stream_one_bf):
        active, slope = gelu_pair(mm(stream_one_bf, w_up) + b_up)
        result, kept = norm_fwd(
            stream_one + mm(active, w_down) + b_down, gains[1], shifts[1], EPS_MODEL
        )
        return result.astype(BF), active, slope, kept

    def feed_back(grad_result, slope, kept):
        grad_two, gain_two, shift_two = norm_bwd(grad_result, kept, gains[1])
        grad_f = grad_two.astype(BF)
        grad_h = (mm_rt(grad_f, w_down) * slope.astype(F32)).astype(BF)
        return grad_f, grad_h, grad_two + mm_rt(grad_h, w_up), gain_two, shift_two

    def blank(shapes):
        return jax.tree.map(lambda s: jnp.zeros(s.shape, s.dtype), shapes)

    def when(flag, work):
        return lax.cond(flag, work, lambda: blank(jax.eval_shape(work)))

    enc_out, enc_active, enc_slope, enc_kept = when(is_enc, lambda: feed(first, first_bf))
    (enc_out,) = stage(enc_out)
    memory_low = links.to_dec(enc_out)
    (memory_low,) = stage(memory_low)

    cross_off = (0, 0, width)

    def decoder_branch():
        w_cq = cross_full[:, :width]
        w_ckv = cross_full[:, width : 3 * width]
        w_co = cross_full[:, 3 * width : 4 * width]
        cross_small = cross_full[:, 4 * width :]
        cross_small = cross_small.reshape(2 * n, -1).astype(F32)
        cb_q, cb_v, cb_o, c_gain, c_shift = vectors_of(cross_small, cross_vecs)
        cq = (mm(first_bf, w_cq) + cb_q).astype(BF)
        bias_kv = jnp.concatenate([jnp.zeros((width,), F32), cb_v])
        ckv = (mm(memory_low, w_ckv) + bias_kv).astype(BF)
        cmixed = attend(cq, ckv, ckv, cross_off, width, labels, plain)
        second, kept_cross = norm_fwd(
            first + mm(cmixed, w_co) + cb_o, c_gain, c_shift, EPS_MODEL
        )
        second_bf = second.astype(BF)
        decoded, active, slope, kept = feed(second, second_bf)
        grad_f, grad_h, grad_second, gain_two, shift_two = feed_back(
            adjoint_bf.astype(F32), slope, kept
        )
        grad_cross, cgain, cshift = norm_bwd(grad_second, kept_cross, c_gain)
        grad_cross_bf = grad_cross.astype(BF)
        grad_cmixed = mm_rt(grad_cross_bf, w_co).astype(BF)
        grad_cq, grad_ckv = attend_back(
            cq, ckv, ckv, cross_off, width, labels, plain, grad_cmixed, False
        )
        grad_memory = mm_rt(grad_ckv, w_ckv).astype(BF)
        cross_small_grads = (
            colsum(grad_cq),
            colsum(grad_ckv[:, width:]),
            colsum(grad_cross_bf),
            cgain,
            cshift,
        )
        return (
            decoded,
            grad_memory,
            second_bf,
            active,
            grad_f,
            grad_h,
            (gain_two, shift_two),
            cross_small_grads,
            (grad_cross, grad_cross_bf, cmixed, grad_cq, grad_ckv),
        )

    shapes = jax.eval_shape(decoder_branch)
    dec = lax.cond(
        is_enc,
        lambda: (enc_out, jnp.zeros((total, width), BF), first_bf, enc_active) + blank(shapes[4:]),
        decoder_branch,
    )
    (
        layer_rows, grad_memory, feed_in, active, dec_f, dec_h, dec_norm, cross_small_grads, cross_kept
    ) = dec
    grad_memory, cross_kept, query_full = stage(grad_memory, cross_kept, query_full)

    passages = document_vectors.shape[1]
    n_span, n_pick = micro * asked, micro * asked * chosen_count

    def query_branch():
        tail = doc_packet[micro * passages]
        spans = tail[:n_span].astype(jnp.int32).reshape(micro, asked)
        slots = tail[n_span : n_span + n_pick].astype(jnp.int32).reshape(micro, asked, chosen_count)
        adjoint = tail[n_span + n_pick : n_span + 2 * n_pick].reshape(n_span, chosen_count)
        base = jnp.arange(micro, dtype=jnp.int32)[:, None]
        per_block = inquiry_vectors.shape[1]
        ends = jnp.cumsum(spans, axis=1)
        firsts = (ends - spans + base * per_block).reshape(-1)
        ends = (ends + base * per_block).reshape(-1)
        where_doc = (slots + base[:, :, None] * passages).reshape(n_span, chosen_count)
        query_small = query_full[:, 4 * q_width + 2 * q_ff :].reshape(2 * n, -1).astype(F32)
        return query_work(
            q_block_rows,
            firsts,
            ends,
            doc_packet[where_doc],
            adjoint,
            heat,
            query_full,
            q_ff,
            2 * n,
            vectors_of(query_small, query_vecs),
        )

    queried = when(is_enc, query_branch)
    memory_grad = links.to_enc(grad_memory)

    def cross_late():
        grad_cross, grad_cross_bf, cmixed, grad_cq, grad_ckv = cross_kept
        grads = jnp.concatenate(
            [
                mm_lt(first_bf, grad_cq).astype(BF),
                mm_lt(memory_low, grad_ckv).astype(BF),
                mm_lt(cmixed, grad_cross_bf).astype(BF),
            ],
            axis=1,
        )
        return grads, grad_cross + mm_rt(grad_cq, cross_full[:, :width])

    cross_grads, dec_first = lax.cond(
        is_enc,
        lambda: (jnp.zeros((width, 4 * width), BF), jnp.zeros((total, width), F32)),
        cross_late,
    )
    scored, q_grad_rows, grad_heat, query_grads, query_small_grads = queried
    half_rows = query_grads.shape[0] // 2
    factors_got = links.to_dec(query_grads[half_rows:])
    memory_grad, cross_grads, dec_first, query_grads, factors_got = stage(
        memory_grad, cross_grads, dec_first, query_grads, factors_got
    )
    factors = lax.all_gather(
        jnp.where(is_enc, query_grads[:half_rows], factors_got), everyone, axis=0, tiled=True
    )

    def enc_back():
        grad_f, grad_h, grad_first, gain_two, shift_two = feed_back(
            memory_grad.astype(F32), enc_slope, enc_kept
        )
        return grad_f, grad_h, grad_first, (gain_two, shift_two)

    grad_f, grad_h, grad_first, norm_two = lax.cond(
        is_enc, enc_back, lambda: (dec_f, dec_h, dec_first, dec_norm)
    )

    grad_h, grad_f, grad_first, layer_rows = stage(grad_h, grad_f, grad_first, layer_rows)
    layer_home = links.swap(layer_rows)
    up_got = links.reduce_open(feed_in, grad_h)
    down_got = links.reduce_open(active, grad_f)
    cross_pair = cross_grads.reshape(2, width // 2, 4 * width)
    cross_got = links.flip(
        lax.dynamic_index_in_dim(cross_pair, 1 - core, 0, keepdims=False), "dec"
    )
    grad_one, gain_one, shift_one = norm_bwd(grad_first, kept_one, gains[0])
    grad_one_bf = grad_one.astype(BF)
    grad_mixed = mm_rt(grad_one_bf, w_out).astype(BF)
    up_got, down_got, cross_got, grad_mixed, layer_home = stage(
        up_got, down_got, cross_got, grad_mixed, layer_home
    )
    cross_sum = lax.dynamic_index_in_dim(cross_pair, core, 0, keepdims=False)
    cross_sum = (cross_sum.astype(F32) + cross_got.astype(F32)).astype(BF)
    cross_sum = cross_sum.reshape((2,) + (2,) * links.bits + (cross_rows, 4 * width))
    cross_sum = links.reduce_step(cross_sum, 0, 0, "dec", 1)
    up_sum = links.reduce_step(links.reduce_own(feed_in, grad_h, up_got), 1, 0)
    down_sum = links.reduce_step(links.reduce_own(active, grad_f, down_got), 2, 0)
    grad_joint = attend_back(
        joint, joint, joint, self_off, width, labels, causal, grad_mixed, True
    )
    up_sum, down_sum, cross_sum, grad_joint, factors = stage(
        up_sum, down_sum, cross_sum, grad_joint, factors
    )
    device = core * n + links.dp

    def own_columns(matrix, count):
        wide = matrix.shape[1]
        lines = lax.broadcasted_iota(jnp.int32, (wide, count), 0)
        places = lax.broadcasted_iota(jnp.int32, (wide, count), 1) + device * count
        return mm(matrix, (lines == places).astype(BF)).astype(BF)

    all_asked = 2 * n * asked
    seen_keys = own_columns(factors[:, :q_width], q_rows).reshape(all_asked, QHEADS, q_rows)
    seen_values = own_columns(factors[:, q_width : 2 * q_width], q_rows)
    seen_values = seen_values.reshape(all_asked, QHEADS, q_rows)
    factors = factors[:, 2 * q_width :].reshape(all_asked, -1)
    sizes, at, cols = [q_width] * 5 + [q_ff, q_ff] + [q_width] * 3, 0, []
    for size in sizes:
        cols.append(factors[:, at : at + size])
        at += size
    f_head, f_q, f_mixed, f_one, f_middle, f_hidden, f_active, f_two, f_asks, f_gmix = cols

    def by_head(seen, other, scale):
        per_head = jnp.einsum(
            "qhd,qhe->hde", seen, heads_of(other, QHEADS), preferred_element_type=F32
        )
        return per_head.transpose(1, 0, 2).reshape(q_rows, q_width) * scale

    query_k_own = by_head(seen_keys, f_asks, (q_width // QHEADS) ** (-0.5))
    query_v_own = by_head(seen_values, f_gmix, 1.0)
    query_q_own = mm_lt(own_columns(f_head, q_rows), f_q)
    query_out_own = mm_lt(own_columns(f_mixed, q_rows), f_one)
    query_up_own = mm_lt(own_columns(f_middle, q_rows), f_hidden)
    query_down_own = mm_lt(own_columns(f_active, q_rows * q_folds), f_two)
    cross_sum = links.reduce_step(cross_sum, 0, 1, "dec", 1)
    split_joint = [(0, joint_w // 2), (joint_w // 2, joint_w)]
    attn_jobs = [(stream_bf, grad_joint[:, a:b]) for a, b in split_joint]
    attn_jobs += [(mixed, grad_one_bf)]
    attn_got = [links.reduce_open(left, right) for left, right in attn_jobs]
    grad_rows = (grad_one + mm_rt(grad_joint, w_joint)).astype(BF)
    query_own_mats = [
        jnp.concatenate([query_q_own, query_k_own, query_v_own], axis=1),
        query_out_own,
        query_up_own,
        query_down_own,
    ]
    up_sum = links.reduce_step(up_sum, 1, 1)
    down_sum = links.reduce_step(down_sum, 2, 1)

    def role_rows(vec):
        return vec.reshape(n, -1)

    def role_pair_rows(one, two):
        return jnp.stack([role_rows(one), role_rows(two)], axis=1).reshape(n, -1)

    def side_rows(vec):
        lead = vec.reshape(-1, vec.shape[-1]).shape[0]
        return vec.reshape(lead, 2 * n, -1).transpose(1, 0, 2).reshape(2 * n, -1)

    joint_cols = colsum(grad_joint)
    role_grads = jnp.concatenate(
        [
            role_rows(jnp.concatenate([joint_cols[:width], joint_cols[2 * width :]])),
            role_rows(colsum(grad_one_bf)),
            role_rows(colsum(grad_h)),
            role_rows(colsum(grad_f)),
            role_pair_rows(gain_one, norm_two[0]),
            role_pair_rows(shift_one, norm_two[1]),
        ],
        axis=-1,
    )
    def lead_rows(table):
        table = table.reshape(2, 2, half, -1).transpose(0, 2, 1, 3)
        return table.reshape(2, half, -1)

    cross_table = jnp.concatenate([side_rows(v) for v in cross_small_grads], axis=1)
    query_table = jnp.concatenate([side_rows(v) for v in query_small_grads], axis=1)
    small_grads = jnp.concatenate(
        [
            role_grads.reshape(2, half, n_role),
            lead_rows(cross_table),
            lead_rows(query_table),
            jnp.broadcast_to(grad_heat, (2, half, 1)),
        ],
        axis=2,
    )
    small_sum = lax.dynamic_index_in_dim(small_grads, core, 0, keepdims=False)
    small_got = links.flip(lax.dynamic_index_in_dim(small_grads, 1 - core, 0, keepdims=False))
    small_sum = (small_sum + small_got).reshape((2,) * links.bits + (1, -1))
    up_sum, down_sum, cross_sum, attn_got, grad_rows, small_sum = stage(
        up_sum, down_sum, cross_sum, attn_got, grad_rows, small_sum
    )
    rows_home = links.swap(grad_rows)
    for step in range(2, links.bits):
        up_sum = links.reduce_step(up_sum, 1, step)
        down_sum = links.reduce_step(down_sum, 2, step)
        cross_sum = links.reduce_step(cross_sum, 0, step, "dec", 1)
    attn_sum = [
        links.reduce_step(links.reduce_own(left, right, got), turn, 0)
        for turn, ((left, right), got) in enumerate(zip(attn_jobs, attn_got))
    ]
    small_sum = links.reduce_step(small_sum, 0, 0)
    attn_sum, up_sum, down_sum, rows_home, small_sum, cross_sum, query_own_mats = stage(
        attn_sum, up_sum, down_sum, rows_home, small_sum, cross_sum, query_own_mats
    )
    up_own = links.swap(up_sum.reshape(-1, ff)).astype(F32)
    down_own = links.swap(down_sum.reshape(-1, width)).astype(F32)
    for step in range(1, links.bits):
        attn_sum = [links.reduce_step(v, turn, step) for turn, v in enumerate(attn_sum)]
        small_sum = links.reduce_step(small_sum, 0, step)
        if step + 1 < links.bits:
            attn_sum, small_sum = stage(attn_sum, small_sum)
    attn_home = jnp.concatenate([v.reshape(-1, v.shape[-1]) for v in attn_sum], axis=1)
    attn_home = links.swap(attn_home).astype(F32)
    joint_own, out_own = attn_home[:, :joint_w], attn_home[:, joint_w:]
    cross_sum = cross_sum.reshape(2, cross_rows, 4 * width)
    cross_sum = jnp.where(is_enc, links.to_enc(cross_sum[0]), cross_sum[1]).astype(F32)
    cross_own_mats = [
        cross_sum[:, :width],
        cross_sum[:, width : 3 * width],
        cross_sum[:, 3 * width :],
    ]
    small_sum = small_sum.reshape(-1)
    role_own = links.swap(small_sum[:n_role])
    cross_pair = small_sum[n_role : n_role + 2 * n_cross].reshape(2, n_cross)
    query_pair = small_sum[n_role + 2 * n_cross : n_role + 2 * n_cross + 2 * n_query]
    pairs = jnp.concatenate([cross_pair, query_pair.reshape(2, n_query)], axis=1)
    keep_side = jnp.concatenate([jnp.where(is_enc, pairs[0], pairs[1]), small_sum[-1:]])
    send_side = jnp.concatenate([jnp.where(is_enc, pairs[1], pairs[0]), small_sum[-1:]])
    side_own = keep_side + links.across(send_side)
    cross_own = side_own[:n_cross]
    query_own = side_own[n_cross : n_cross + n_query]
    heat_total = side_own[-1:]

    layer_out = layer_home.reshape(1, micro, rows, width)
    input_grad = rows_home.astype(F32).reshape(1, micro, rows, width)

    per_block = inquiry_vectors.shape[1]
    score_row = jnp.pad(scored.reshape(1, -1), ((0, 0), (0, q_width - scored.size))).astype(BF)
    q_packet = jnp.concatenate([q_grad_rows.astype(BF), score_row])
    up_mark, q_packet = stage(up_own, q_packet)
    q_home = links.home_enc(q_packet)
    q_mats = q_home[: micro * per_block].reshape(micro, per_block, q_width)
    s_mats = q_home[micro * per_block :, : scored.size].reshape(micro, 1, -1)
    second = jnp.concatenate(
        [q_mats[1], jnp.pad(s_mats[1], ((0, 0), (0, q_width - s_mats.shape[2])))]
    )
    got_second = lax.ppermute(second, "phase", [(0, 1)])
    question_grad = jnp.where(core == 0, q_mats[0], got_second[:per_block]).astype(F32)[None]
    own_scores = jnp.where(core == 0, s_mats[0], got_second[per_block:, : s_mats.shape[2]])
    scores = own_scores.astype(F32).reshape(1, asked, chosen_count)

    sizes = [
        intrinsic_probe_content_offset.shape[1],
        intrinsic_mixing_result_offset.shape[1],
        perceptron_widen_offset.shape[1],
        perceptron_narrow_offset.shape[1],
        2 * standardize_scales.shape[2],
        2 * standardize_shifts.shape[2],
    ]
    cut, role_out = 0, []
    for size in sizes:
        role_out.append(role_own[cut : cut + size])
        cut += size
    role_tuple = (
        joint_own[None],
        role_out[0][None],
        out_own[None],
        role_out[1][None],
        up_own[None],
        role_out[2][None],
        down_own[None],
        role_out[3][None],
        role_out[4].reshape(1, 2, -1),
        role_out[5].reshape(1, 2, -1),
    )
    c = cross_own.reshape(5, -1)
    cross_tuple = (
        cross_own_mats[0],
        c[0],
        cross_own_mats[1],
        c[1],
        cross_own_mats[2],
        c[2],
        c[3],
        c[4],
    )
    cut, q_out = 0, []
    for part in (
        retriever_probe_content_offset,
        retriever_mixing_result_offset,
        retriever_widen_offset,
        retriever_narrow_offset,
        retriever_standardize_scales,
        retriever_standardize_shifts,
    ):
        q_out.append(query_own[cut : cut + part.size].reshape(part.shape))
        cut += part.size
    query_tuple = (
        query_own_mats[0],
        q_out[0],
        query_own_mats[1],
        q_out[1],
        query_own_mats[2],
        q_out[2],
        query_own_mats[3],
        q_out[3],
        q_out[4],
        q_out[5],
    )
    return (
        (layer_out, input_grad, scores, question_grad, heat_total)
        + role_tuple
        + cross_tuple
        + query_tuple
    )


def solution(mesh):
    row = P(None, "dp", None)
    mat, vec = P("phase", "dp", None), P("phase", "dp")
    pair = P("phase", None, "dp")
    side_mat, side_vec = P(("phase", "dp"), None), P(("phase", "dp"))
    side_pair = P(None, ("phase", "dp"))
    role = (mat, vec, mat, vec, mat, vec, mat, vec, pair, pair)
    cross = (side_mat, side_vec, side_mat, side_vec, side_mat, side_vec, side_vec, side_vec)
    query = (side_mat, side_vec) * 4 + (side_pair, side_pair)
    stream = P("phase", None, "dp", None)
    in_specs = (stream,) + (row,) * 7 + (P(),) + role + cross + query
    out_specs = (stream, stream, mat, mat, P()) + role + cross + query
    return jax.shard_map(local, mesh=mesh, in_specs=in_specs, out_specs=out_specs, check_vma=False)
```

```python
from functools import partial

import jax
import jax.numpy as jnp
from jax import lax
from jax.experimental import pallas as pl
from jax.experimental.pallas import tpu as pltpu
from jax.sharding import PartitionSpec as P

HEADS = 16
QHEADS = 12
NEG_FILL = -1e30
EPS_MODEL = 1e-05
EPS_QUERY = 1e-12
BF = jnp.bfloat16
F32 = jnp.float32


def mm(left, right):
    return jnp.dot(left, right, preferred_element_type=F32)


def mm_lt(left, right):
    return lax.dot_general(left, right, (((0,), (0,)), ((), ())), preferred_element_type=F32)


def mm_rt(left, right):
    return lax.dot_general(left, right, (((1,), (1,)), ((), ())), preferred_element_type=F32)


def colsum(matrix):
    return jnp.sum(matrix.astype(F32), axis=0)


def norm_fwd(stream, gain, bias, eps):
    centred = stream - jnp.mean(stream, axis=-1, keepdims=True)
    rstd = lax.rsqrt(jnp.mean(centred * centred, axis=-1, keepdims=True) + eps)
    hat = centred * rstd
    return hat * gain + bias, (hat, rstd)


def norm_bwd(grad, kept, gain):
    hat, rstd = kept
    scaled = grad * gain
    centre = jnp.mean(scaled, axis=-1, keepdims=True)
    along = jnp.mean(scaled * hat, axis=-1, keepdims=True)
    return rstd * (scaled - centre - hat * along), jnp.sum(grad * hat, axis=0), jnp.sum(grad, axis=0)


def gelu_pair(hidden):
    cdf = 0.5 * (1.0 + lax.erf(hidden * 0.7071067811865476))
    pdf = jnp.exp(-0.5 * hidden * hidden) * 0.3989422804014327
    return (hidden * cdf).astype(BF), (cdf + hidden * pdf).astype(BF)


def allowed_bias(key_ref, query_ref, causal_ref):
    same = key_ref[0] == query_ref[0]
    keys = lax.broadcasted_iota(jnp.int32, same.shape, 0)
    queries = lax.broadcasted_iota(jnp.int32, same.shape, 1)
    seen = jnp.logical_and(same, jnp.logical_or(queries >= keys, causal_ref[0] == 0))
    return jnp.where(seen, 0.0, NEG_FILL).astype(F32)


def attn_fwd_body(
    head_size, q_off, k_off, v_off, causal_ref, key_ref, query_ref, q_ref, k_ref, v_ref, o_ref
):
    bias = allowed_bias(key_ref, query_ref, causal_ref)
    scale = head_size ** (-0.5)
    pairs = o_ref.shape[1] // 128

    def one(pair, carry):
        at = pl.multiple_of(pair * 128, 128)
        q2 = q_ref[:, pl.ds(q_off + at, 128)]
        q2 = (q2.astype(F32) * scale).astype(BF)
        k2 = k_ref[:, pl.ds(k_off + at, 128)]
        v_t = v_ref[:, pl.ds(v_off + at, 128)].T
        lane = lax.broadcasted_iota(jnp.int32, q2.shape, 1) < head_size
        mixed = []
        for mine in (lane, jnp.logical_not(lane)):
            scores = mm_rt(k2, jnp.where(mine, q2, jnp.zeros_like(q2))) + bias
            raised = jnp.exp(scores - jnp.max(scores, axis=0, keepdims=True))
            total = jnp.sum(raised, axis=0, keepdims=True)
            mixed.append(mm(v_t, raised.astype(BF)) * (1.0 / total))
        row = lax.broadcasted_iota(jnp.int32, mixed[0].shape, 0) < head_size
        o_ref[:, pl.ds(at, 128)] = jnp.where(row, mixed[0], mixed[1]).T.astype(BF)
        return carry

    lax.fori_loop(0, pairs, one, 0)


def attn_bwd_body(
    head_size, q_off, k_off, v_off, joint, causal_ref, key_ref, query_ref, q_ref, k_ref, v_ref, g_ref, *outs
):
    bias = allowed_bias(key_ref, query_ref, causal_ref)
    scale = head_size ** (-0.5)
    pairs = g_ref.shape[1] // 128
    dq_ref, dk_ref, dv_ref = (outs[0],) * 3 if joint else (outs[0], outs[1], outs[1])

    def one(pair, carry):
        at = pl.multiple_of(pair * 128, 128)
        q2 = q_ref[:, pl.ds(q_off + at, 128)]
        q2 = (q2.astype(F32) * scale).astype(BF)
        k2 = k_ref[:, pl.ds(k_off + at, 128)]
        v2 = v_ref[:, pl.ds(v_off + at, 128)]
        g2 = g_ref[:, pl.ds(at, 128)]
        k_t = k2.T
        lane = lax.broadcasted_iota(jnp.int32, q2.shape, 1) < head_size
        parts = []
        for mine in (lane, jnp.logical_not(lane)):
            scores = mm_rt(k2, jnp.where(mine, q2, jnp.zeros_like(q2))) + bias
            raised = jnp.exp(scores - jnp.max(scores, axis=0, keepdims=True))
            chances = raised * (1.0 / jnp.sum(raised, axis=0, keepdims=True))
            grad_p = mm_rt(v2, jnp.where(mine, g2, jnp.zeros_like(g2)))
            inner = jnp.sum(chances * grad_p, axis=0, keepdims=True)
            grad_s = (chances * (grad_p - inner)).astype(BF)
            grad_v = mm(chances.astype(BF), g2)
            grad_k = mm(grad_s, q2)
            grad_q_t = mm(k_t, grad_s)
            parts.append((grad_q_t, grad_k, grad_v))
        row = lax.broadcasted_iota(jnp.int32, parts[0][0].shape, 0) < head_size
        grad_q = jnp.where(row, parts[0][0], parts[1][0]).T * scale
        dq_ref[:, pl.ds(q_off + at, 128)] = grad_q.astype(BF)
        dk_ref[:, pl.ds(k_off + at, 128)] = jnp.where(lane, parts[0][1], parts[1][1]).astype(BF)
        dv_ref[:, pl.ds(v_off + at, 128)] = jnp.where(lane, parts[0][2], parts[1][2]).astype(BF)
        return carry

    lax.fori_loop(0, pairs, one, 0)


def attn_specs(rows, arrays):
    specs = [
        pl.BlockSpec(memory_space=pltpu.SMEM),
        pl.BlockSpec((1, rows, 1), lambda m: (m, 0, 0)),
        pl.BlockSpec((1, 1, rows), lambda m: (m, 0, 0)),
    ]
    return specs + [pl.BlockSpec((rows, a.shape[1]), lambda m: (m, 0)) for a in arrays]


def attn_params():
    return pltpu.CompilerParams(dimension_semantics=("arbitrary",), vmem_limit_bytes=48 << 20)


def attn_cost(total, rows, width, products):
    return pl.CostEstimate(
        flops=2 * products * total * rows * width,
        transcendentals=total * rows * HEADS,
        bytes_accessed=total * width * 2 * (4 if products == 2 else 7),
    )


def attend(q, k, v, offsets, width, labels, causal):
    rows = labels.shape[1]
    total = q.shape[0]
    return pl.pallas_call(
        partial(attn_fwd_body, width // HEADS, *offsets),
        grid=(total // rows,),
        in_specs=attn_specs(rows, (q, k, v)),
        out_specs=pl.BlockSpec((rows, width), lambda m: (m, 0)),
        out_shape=jax.ShapeDtypeStruct((total, width), BF),
        compiler_params=attn_params(),
        cost_estimate=attn_cost(total, rows, width, 2),
        name="attend_fwd",
    )(causal, labels[:, :, None], labels[:, None, :], q, k, v)


def attend_back(q, k, v, offsets, width, labels, causal, grad, joint):
    rows = labels.shape[1]
    total = q.shape[0]
    widths = (3 * width,) if joint else (width, 2 * width)
    out = pl.pallas_call(
        partial(attn_bwd_body, width // HEADS, *offsets, joint),
        grid=(total // rows,),
        in_specs=attn_specs(rows, (q, k, v, grad)),
        out_specs=[pl.BlockSpec((rows, w), lambda m: (m, 0)) for w in widths],
        out_shape=[jax.ShapeDtypeStruct((total, w), BF) for w in widths],
        compiler_params=attn_params(),
        cost_estimate=attn_cost(total, rows, width, 5),
        name="attend_bwd",
    )(causal, labels[:, :, None], labels[:, None, :], q, k, v, grad)
    return out[0] if joint else tuple(out)


def heads_of(matrix, count):
    return matrix.reshape(matrix.shape[0], count, matrix.shape[1] // count)


def query_work(
    rows_bf, firsts, ends, chosen, adjoint, heat, sheet, hidden_size, shards, vectors
):
    b_joint, b_out, b_up, b_down, gains, shifts = vectors
    width = rows_bf.shape[1]
    folds = hidden_size // width
    w_joint = sheet[:, : 3 * width]
    w_out = sheet[:, 3 * width : 4 * width]
    w_up = sheet[:, 4 * width : 4 * width + hidden_size]
    downs = [
        sheet[:, 4 * width + hidden_size + i * width : 5 * width + hidden_size + i * width]
        for i in range(folds)
    ]

    def fold(matrix):
        split = matrix.reshape(matrix.shape[0], shards, folds, -1)
        return [split[:, :, i].reshape(matrix.shape[0], width) for i in range(folds)]

    def unfold(parts):
        split = [p.reshape(p.shape[0], shards, 1, -1) for p in parts]
        return jnp.concatenate(split, axis=2).reshape(parts[0].shape[0], -1)

    scale = (width // QHEADS) ** (-0.5)
    positions = jnp.arange(rows_bf.shape[0], dtype=jnp.int32)
    allowed = (positions[None, :] >= firsts[:, None]) & (positions[None, :] < ends[:, None])
    pick = (positions[None, :] == firsts[:, None]).astype(BF)
    head_bf = mm(pick, rows_bf).astype(BF)
    queries = (mm(head_bf, w_joint[:, :width]) + b_joint[:width]).astype(BF)
    paired = mm(rows_bf, w_joint[:, width:])
    keys = paired[:, :width].astype(BF)
    values = (paired[:, width:] + b_joint[width:]).astype(BF)
    qh, kh, vh = heads_of(queries, QHEADS), heads_of(keys, QHEADS), heads_of(values, QHEADS)
    scores = jnp.einsum("qhd,khd->hqk", qh, kh, preferred_element_type=F32) * scale
    scores = jnp.where(allowed[None], scores, NEG_FILL)
    chances = jax.nn.softmax(scores, axis=-1)
    chances_bf = chances.astype(BF)
    mixed = jnp.einsum("hqk,khd->qhd", chances_bf, vh, preferred_element_type=F32)
    mixed = mixed.reshape(queries.shape).astype(BF)
    branch = mm(mixed, w_out) + b_out
    middle, kept_one = norm_fwd(head_bf.astype(F32) + branch, gains[0], shifts[0], EPS_QUERY)
    middle_bf = middle.astype(BF)
    active, slope = gelu_pair(mm(middle_bf, w_up) + b_up)
    folded = fold(active)
    fed = sum(mm(part, down) for part, down in zip(folded, downs))
    found, kept_two = norm_fwd(middle + fed + b_down, gains[1], shifts[1], EPS_QUERY)
    raw = jnp.sum(found[:, None, :] * chosen, axis=-1)
    scored = raw / heat
    grad_heat = -jnp.sum(adjoint * raw) / (heat * heat)
    grad_found = jnp.sum((adjoint / heat)[:, :, None] * chosen, axis=1)
    grad_two, gain_two, shift_two = norm_bwd(grad_found, kept_two, gains[1])
    grad_two_bf = grad_two.astype(BF)
    grad_active = unfold([mm_rt(grad_two_bf, down) for down in downs])
    grad_hidden = (grad_active * slope.astype(F32)).astype(BF)
    grad_middle = grad_two + mm_rt(grad_hidden, w_up)
    grad_one, gain_one, shift_one = norm_bwd(grad_middle, kept_one, gains[0])
    grad_one_bf = grad_one.astype(BF)
    grad_mixed = heads_of(mm_rt(grad_one_bf, w_out).astype(BF), QHEADS)
    grad_values = jnp.einsum("hqk,qhd->khd", chances_bf, grad_mixed, preferred_element_type=F32)
    grad_chances = jnp.einsum("qhd,khd->hqk", grad_mixed, vh, preferred_element_type=F32)
    inner = jnp.sum(chances * grad_chances, axis=-1, keepdims=True)
    grad_scores = (chances * (grad_chances - inner)).astype(BF)
    grad_q = jnp.einsum("hqk,khd->qhd", grad_scores, kh, preferred_element_type=F32) * scale
    grad_k = jnp.einsum("hqk,qhd->khd", grad_scores, qh, preferred_element_type=F32) * scale
    grad_q = grad_q.reshape(queries.shape).astype(BF)
    grad_kv = jnp.concatenate(
        [grad_k.reshape(keys.shape), grad_values.reshape(keys.shape)], axis=1
    ).astype(BF)
    grad_heads = grad_one + mm_rt(grad_q, w_joint[:, :width])
    spread = lax.dot_general(
        pick.astype(F32), grad_heads, (((0,), (0,)), ((), ())),
        precision=lax.Precision.HIGHEST, preferred_element_type=F32,
    )
    grad_rows = mm_rt(grad_kv, w_joint[:, width:]) + spread
    factors = [
        head_bf, grad_q, mixed, grad_one_bf, middle_bf, grad_hidden, active, grad_two_bf,
        queries, grad_mixed.reshape(queries.shape),
    ]
    seen = [
        jnp.einsum("hqk,kd->qhd", p, rows_bf, preferred_element_type=F32)
        for p in (grad_scores, chances_bf)
    ]
    seen = jnp.concatenate(seen, axis=2).astype(BF).reshape(-1, 2 * width)
    mats = (jnp.concatenate(factors, axis=1), seen)
    smalls = (
        jnp.concatenate([colsum(grad_q), colsum(grad_kv[:, width:])]),
        colsum(grad_one_bf),
        colsum(grad_hidden),
        colsum(grad_two_bf),
        jnp.stack([gain_one, gain_two]),
        jnp.stack([shift_one, shift_two]),
    )
    return scored, grad_rows, grad_heat, mats, smalls


class Links:
    def __init__(self):
        self.n = lax.axis_size("dp")
        self.half = self.n // 2
        self.bits = self.half.bit_length() - 1
        self.core = lax.axis_index("phase")
        self.dp = lax.axis_index("dp")
        self.is_enc = self.dp < self.half

    def all_pairs(self, value, pairs):
        return lax.ppermute(value, ("phase", "dp"), pairs)

    def swap(self, value):
        n, h = self.n, self.half
        pairs = []
        for i in range(h):
            pairs += [(i, i), (n + i, i + h), (i + h, n + i), (n + i + h, n + i + h)]
        return self.all_pairs(value, pairs)

    def pull_enc(self, value):
        n, h = self.n, self.half
        pairs = []
        for i in range(h):
            pairs += [(i, i), (i + h, n + i)]
        return self.all_pairs(value, pairs)

    def home_enc(self, value):
        n, h = self.n, self.half
        pairs = []
        for i in range(h):
            pairs += [(i, i), (n + i, i + h)]
        return self.all_pairs(value, pairs)

    def home_dec(self, value):
        n, h = self.n, self.half
        pairs = []
        for i in range(h):
            pairs += [(n + i + h, n + i + h), (i + h, n + i)]
        return self.all_pairs(value, pairs)

    def push_dec(self, value):
        n, h = self.n, self.half
        pairs = []
        for i in range(h):
            pairs += [(n + i + h, n + i + h), (n + i, i + h)]
        return self.all_pairs(value, pairs)

    def to_dec(self, value):
        return lax.ppermute(value, "dp", [(i, i + self.half) for i in range(self.half)])

    def to_enc(self, value):
        return lax.ppermute(value, "dp", [(i + self.half, i) for i in range(self.half)])

    def across(self, value):
        h = self.half
        pairs = [(i, i + h) for i in range(h)] + [(i + h, i) for i in range(h)]
        return lax.ppermute(value, "dp", pairs)

    def flip(self, value, who="both"):
        first = self.half if who == "dec" else 0
        last = self.half if who == "enc" else self.n
        pairs = []
        for i in range(first, last):
            pairs += [(i, self.n + i), (self.n + i, i)]
        return self.all_pairs(value, pairs)

    def hop(self, value, bit, who):
        first = self.half if who == "dec" else 0
        last = self.half if who == "enc" else self.n
        return lax.ppermute(value, "dp", [(i, i ^ (1 << bit)) for i in range(first, last)])

    def order(self, turn):
        return [(turn + k) % self.bits for k in range(self.bits)]

    def gather_hop(self, held, turn, step, who="both"):
        return self.hop(held, self.order(turn)[step], who)

    def places(self, turn, lead=1):
        order = self.order(turn)
        mine = self.dp % self.half
        masks = [
            sum(((p >> j) & 1) << order[j] for j in range(self.bits)) for p in range(self.half)
        ]
        own = jnp.stack(
            [jnp.bitwise_xor(mine, m) + r * self.half for m in masks for r in range(lead)]
        ).astype(jnp.int32)
        wide = lead * self.half
        return jnp.concatenate([own + self.core * wide, own + (1 - self.core) * wide])

    def half_of(self, left, core):
        wide = left.shape[1] // 2
        return lax.dynamic_slice_in_dim(left, core * wide, wide, 1)

    def reduce_open(self, left, right):
        return self.flip(mm_lt(self.half_of(left, 1 - self.core), right).astype(BF))

    def reduce_own(self, left, right, got):
        own = mm_lt(self.half_of(left, self.core), right) + got.astype(F32)
        shard = left.shape[1] // self.n
        return own.astype(BF).reshape((2,) * self.bits + (shard, right.shape[1]))

    def reduce_steps(self, jobs):
        keeps, gots = [], []
        for value, turn, step, who, lead in jobs:
            bit = self.order(turn)[step]
            mine = (self.dp >> bit) & 1
            axis = lead + self.bits - 1 - bit
            send = lax.dynamic_slice_in_dim(value, 1 - mine, 1, axis)
            keeps.append(lax.dynamic_slice_in_dim(value, mine, 1, axis))
            gots.append(self.hop(send, bit, who))
        gots = lax.optimization_barrier(tuple(gots))
        return [
            (keep.astype(F32) + got.astype(F32)).astype(keep.dtype)
            for keep, got in zip(keeps, gots)
        ]

    def reduce_step(self, value, turn, step, who="both", lead=0):
        bit = self.order(turn)[step]
        mine = (self.dp >> bit) & 1
        axis = lead + self.bits - 1 - bit
        send = lax.dynamic_slice_in_dim(value, 1 - mine, 1, axis)
        keep = lax.dynamic_slice_in_dim(value, mine, 1, axis)
        got = self.hop(send, bit, who)
        return (keep.astype(F32) + got.astype(F32)).astype(value.dtype)


def weave_body(quarter, streams, place_ref, *refs):
    count = len(streams)
    at = pl.program_id(0)
    for index in range(4):

        @pl.when(jnp.logical_and(at >= index * quarter, at < (index + 1) * quarter))
        def _(index=index):
            out = 4 * count
            for stream, widths in enumerate(streams):
                low = 0
                for width in widths:
                    refs[out][...] = refs[4 * stream + index][0, :, low : low + width]
                    low += width
                    out += 1


def weave(streams, places, widths):
    quarter = streams[0][0].shape[0]
    total = 4 * quarter

    def source(part, index):
        return pl.BlockSpec(
            (1,) + part.shape[1:],
            lambda g, place: (jnp.clip(g - index * quarter, 0, quarter - 1), 0, 0),
        )

    def target(rows, width, stream):
        return pl.BlockSpec((rows, width), lambda g, place: (place[stream, g], 0))

    shapes = [
        (parts[0].shape[1], w, i)
        for i, (parts, ws) in enumerate(zip(streams, widths))
        for w in ws
    ]
    moved = sum(4 * p.size for parts in streams for p in parts)
    return pl.pallas_call(
        partial(weave_body, quarter, widths),
        grid_spec=pltpu.PrefetchScalarGridSpec(
            num_scalar_prefetch=1,
            grid=(total,),
            in_specs=[source(p, i) for parts in streams for i, p in enumerate(parts)],
            out_specs=[target(*shape) for shape in shapes],
        ),
        out_shape=[jax.ShapeDtypeStruct((total * r, w), BF) for r, w, _ in shapes],
        compiler_params=pltpu.CompilerParams(
            dimension_semantics=("arbitrary",), vmem_limit_bytes=48 << 20
        ),
        cost_estimate=pl.CostEstimate(flops=0, transcendentals=0, bytes_accessed=moved),
        name="weave",
    )(places, *[p for parts in streams for p in parts])


def stage(*values):
    return lax.optimization_barrier(values)


def block_of(values, rows):
    flat = jnp.concatenate([v.reshape(1, -1).astype(BF) for v in values], axis=1)
    return jnp.pad(flat, ((0, 0), (0, rows * 128 - flat.size))).reshape(rows, 128)


def local(
    token_vectors,
    generation_result_adjoint,
    sequence_labels,
    inquiry_vectors,
    inquiry_token_spans,
    document_vectors,
    document_slots,
    relevance_adjoint,
    softness_scalar,
    intrinsic_triple_map,
    intrinsic_probe_content_offset,
    intrinsic_mixing_result_map,
    intrinsic_mixing_result_offset,
    perceptron_widen_map,
    perceptron_widen_offset,
    perceptron_narrow_map,
    perceptron_narrow_offset,
    standardize_scales,
    standardize_shifts,
    encoded_mixing_probe_map,
    encoded_mixing_probe_offset,
    encoded_lookup_content_map,
    encoded_mixing_content_offset,
    encoded_mixing_result_map,
    encoded_mixing_result_offset,
    encoded_mixing_scale_factor,
    encoded_mixing_scale_shift,
    retriever_triple_map,
    retriever_probe_content_offset,
    retriever_mixing_result_map,
    retriever_mixing_result_offset,
    retriever_widen_map,
    retriever_widen_offset,
    retriever_narrow_map,
    retriever_narrow_offset,
    retriever_standardize_scales,
    retriever_standardize_shifts,
):
    links = Links()
    n, half, is_enc, core = links.n, links.half, links.is_enc, links.core
    micro, rows, width = token_vectors.shape[1:]
    total = micro * rows
    joint_w = intrinsic_triple_map.shape[2]
    ff = perceptron_widen_map.shape[2]
    heat = softness_scalar[0]

    role_vecs = (
        intrinsic_probe_content_offset,
        intrinsic_mixing_result_offset,
        perceptron_widen_offset,
        perceptron_narrow_offset,
        standardize_scales,
        standardize_shifts,
    )
    cross_vecs = (
        encoded_mixing_probe_offset,
        encoded_mixing_content_offset,
        encoded_mixing_result_offset,
        encoded_mixing_scale_factor,
        encoded_mixing_scale_shift,
    )
    query_vecs = (
        retriever_probe_content_offset,
        retriever_mixing_result_offset,
        retriever_widen_offset,
        retriever_narrow_offset,
        retriever_standardize_scales,
        retriever_standardize_shifts,
    )
    n_role = sum(v.size for v in role_vecs)
    n_cross = sum(v.size for v in cross_vecs)
    n_query = sum(v.size for v in query_vecs)
    everyone = ("phase", "dp")
    shard_rows = intrinsic_triple_map.shape[1]
    q_width = inquiry_vectors.shape[2]
    q_ff = retriever_widen_map.shape[1]
    q_rows = retriever_triple_map.shape[0]
    q_folds = q_ff // q_width
    cross_rows = encoded_mixing_probe_map.shape[0]

    def vectors_of(table, like):
        at, out = 0, []
        for vec in like:
            lead = vec.shape[-2] if vec.ndim > 1 and vec.shape[-2] > 1 else 1
            piece = table[:, at : at + vec.size].reshape(table.shape[0], lead, -1)
            piece = piece.transpose(1, 0, 2).reshape(lead, -1)
            out.append(piece if lead > 1 else piece[0])
            at += vec.size
        return out

    attn_in = jnp.concatenate(
        [
            intrinsic_triple_map[0],
            intrinsic_mixing_result_map[0],
            block_of(role_vecs + (sequence_labels,), shard_rows),
        ],
        axis=1,
    )
    held = list(
        stage(
            links.swap(attn_in),
            links.swap(perceptron_widen_map[0]),
            links.swap(perceptron_narrow_map[0]),
        )
    )
    labels = held[0][:, joint_w + width :].reshape(1, -1)[:, n_role : n_role + total]
    labels = labels.astype(jnp.int32).reshape(micro, rows)
    held = [v[None] for v in held]
    tokens_in = token_vectors[0].reshape(total, width)
    adjoint_own = generation_result_adjoint.reshape(total, width)
    query_in = jnp.concatenate(
        [retriever_triple_map, retriever_mixing_result_map, retriever_widen_map]
        + [retriever_narrow_map[i * q_rows : (i + 1) * q_rows] for i in range(q_folds)]
        + [block_of(query_vecs, q_rows)],
        axis=1,
    )
    cross_in = jnp.concatenate(
        [
            encoded_mixing_probe_map,
            encoded_lookup_content_map,
            encoded_mixing_result_map,
            block_of(cross_vecs, cross_rows),
        ],
        axis=1,
    )
    asked = inquiry_token_spans.shape[2]
    chosen_count = document_slots.shape[2]
    ints = jnp.concatenate(
        [
            inquiry_token_spans.reshape(1, -1).astype(F32),
            document_slots.reshape(1, -1).astype(F32),
            relevance_adjoint.reshape(1, -1),
        ],
        axis=1,
    )
    doc_own = jnp.concatenate(
        [
            document_vectors.reshape(-1, q_width),
            jnp.pad(ints, ((0, 0), (0, q_width - ints.size))),
        ]
    )
    q_own = inquiry_vectors.reshape(-1, q_width)
    last = links.bits - 1
    cross_full = lax.all_gather(cross_in, everyone, axis=0, tiled=True)
    for step in range(last):
        held = [
            jnp.concatenate([v, links.gather_hop(v, turn, step)], axis=0)
            for turn, v in enumerate(held)
        ]
        if step == 0:
            (held,) = stage(held)
        else:
            held, cross_full = stage(held, cross_full)
    recv = [links.gather_hop(v, turn, last) for turn, v in enumerate(held)]
    theirs = [links.flip(v) for v in held]
    recv, theirs, query_in, tokens_in = stage(recv, theirs, query_in, tokens_in)
    stream_bf = links.swap(tokens_in)
    query_full = lax.all_gather(query_in, everyone, axis=0, tiled=True)
    got = [links.flip(v) for v in recv]
    w_joint, w_out, w_small, w_up, w_down = weave(
        list(zip(held, recv, theirs, got)),
        jnp.stack([links.places(turn) for turn in range(3)]),
        ((joint_w, width, 128), (ff,), (width,)),
    )
    mine_small = w_small.reshape(n, -1)[:, :n_role].astype(F32)
    b_joint, b_out, b_up, b_down, gains, shifts = vectors_of(mine_small, role_vecs)

    causal = jnp.where(is_enc, 0, 1).astype(jnp.int32).reshape(1)
    plain = jnp.zeros((1,), jnp.int32)
    stream = stream_bf.astype(F32)
    bias_joint = jnp.concatenate([b_joint[:width], jnp.zeros((width,), F32), b_joint[width:]])
    joint = (mm(stream_bf, w_joint) + bias_joint).astype(BF)
    self_off = (0, width, 2 * width)
    joint, adjoint_own, doc_own, q_own = stage(joint, adjoint_own, doc_own, q_own)
    adjoint_bf = links.push_dec(adjoint_own)
    doc_packet = links.pull_enc(doc_own)
    q_block_rows = links.pull_enc(q_own)
    mixed = attend(joint, joint, joint, self_off, width, labels, causal)
    first, kept_one = norm_fwd(stream + mm(mixed, w_out) + b_out, gains[0], shifts[0], EPS_MODEL)
    first_bf = first.astype(BF)
    first, first_bf, kept_one, adjoint_bf, doc_packet, q_block_rows = stage(
        first, first_bf, kept_one, adjoint_bf, doc_packet, q_block_rows
    )

    def feed(stream_one, stream_one_bf):
        active, slope = gelu_pair(mm(stream_one_bf, w_up) + b_up)
        result, kept = norm_fwd(
            stream_one + mm(active, w_down) + b_down, gains[1], shifts[1], EPS_MODEL
        )
        return result.astype(BF), active, slope, kept

    def feed_back(grad_result, slope, kept):
        grad_two, gain_two, shift_two = norm_bwd(grad_result, kept, gains[1])
        grad_f = grad_two.astype(BF)
        grad_h = (mm_rt(grad_f, w_down) * slope.astype(F32)).astype(BF)
        return grad_f, grad_h, grad_two + mm_rt(grad_h, w_up), gain_two, shift_two

    def blank(shapes):
        return jax.tree.map(lambda s: jnp.zeros(s.shape, s.dtype), shapes)

    def when(flag, work):
        return lax.cond(flag, work, lambda: blank(jax.eval_shape(work)))

    enc_out, enc_active, enc_slope, enc_kept = when(is_enc, lambda: feed(first, first_bf))
    (enc_out,) = stage(enc_out)
    memory_low = links.to_dec(enc_out)
    (memory_low,) = stage(memory_low)

    cross_off = (0, 0, width)

    def decoder_branch():
        w_cq = cross_full[:, :width]
        w_ckv = cross_full[:, width : 3 * width]
        w_co = cross_full[:, 3 * width : 4 * width]
        cross_small = cross_full[:, 4 * width :]
        cross_small = cross_small.reshape(2 * n, -1).astype(F32)
        cb_q, cb_v, cb_o, c_gain, c_shift = vectors_of(cross_small, cross_vecs)
        cq = (mm(first_bf, w_cq) + cb_q).astype(BF)
        bias_kv = jnp.concatenate([jnp.zeros((width,), F32), cb_v])
        ckv = (mm(memory_low, w_ckv) + bias_kv).astype(BF)
        cmixed = attend(cq, ckv, ckv, cross_off, width, labels, plain)
        second, kept_cross = norm_fwd(
            first + mm(cmixed, w_co) + cb_o, c_gain, c_shift, EPS_MODEL
        )
        second_bf = second.astype(BF)
        decoded, active, slope, kept = feed(second, second_bf)
        grad_f, grad_h, grad_second, gain_two, shift_two = feed_back(
            adjoint_bf.astype(F32), slope, kept
        )
        grad_cross, cgain, cshift = norm_bwd(grad_second, kept_cross, c_gain)
        grad_cross_bf = grad_cross.astype(BF)
        grad_cmixed = mm_rt(grad_cross_bf, w_co).astype(BF)
        grad_cq, grad_ckv = attend_back(
            cq, ckv, ckv, cross_off, width, labels, plain, grad_cmixed, False
        )
        grad_memory = mm_rt(grad_ckv, w_ckv).astype(BF)
        cross_small_grads = (
            colsum(grad_cq),
            colsum(grad_ckv[:, width:]),
            colsum(grad_cross_bf),
            cgain,
            cshift,
        )
        return (
            decoded,
            grad_memory,
            second_bf,
            active,
            grad_f,
            grad_h,
            (gain_two, shift_two),
            cross_small_grads,
            (grad_cross, grad_cross_bf, cmixed, grad_cq, grad_ckv),
        )

    shapes = jax.eval_shape(decoder_branch)
    dec = lax.cond(
        is_enc,
        lambda: (enc_out, jnp.zeros((total, width), BF), first_bf, enc_active) + blank(shapes[4:]),
        decoder_branch,
    )
    (
        layer_rows, grad_memory, feed_in, active, dec_f, dec_h, dec_norm, cross_small_grads, cross_kept
    ) = dec
    grad_memory, cross_kept, query_full, layer_rows = stage(
        grad_memory, cross_kept, query_full, layer_rows
    )

    passages = document_vectors.shape[1]
    n_span, n_pick = micro * asked, micro * asked * chosen_count

    def query_branch():
        tail = doc_packet[micro * passages]
        spans = tail[:n_span].astype(jnp.int32).reshape(micro, asked)
        slots = tail[n_span : n_span + n_pick].astype(jnp.int32).reshape(micro, asked, chosen_count)
        adjoint = tail[n_span + n_pick : n_span + 2 * n_pick].reshape(n_span, chosen_count)
        base = jnp.arange(micro, dtype=jnp.int32)[:, None]
        per_block = inquiry_vectors.shape[1]
        ends = jnp.cumsum(spans, axis=1)
        firsts = (ends - spans + base * per_block).reshape(-1)
        ends = (ends + base * per_block).reshape(-1)
        where_doc = (slots + base[:, :, None] * passages).reshape(n_span, chosen_count)
        query_small = query_full[:, 4 * q_width + 2 * q_ff :].reshape(2 * n, -1).astype(F32)
        return query_work(
            q_block_rows,
            firsts,
            ends,
            doc_packet[where_doc],
            adjoint,
            heat,
            query_full,
            q_ff,
            2 * n,
            vectors_of(query_small, query_vecs),
        )

    queried = when(is_enc, query_branch)
    memory_grad = links.to_enc(grad_memory)
    queried, layer_rows = stage(queried, layer_rows)
    factors_got = [links.to_dec(g[g.shape[0] // 2 :]) for g in queried[3]]
    enc_home = links.home_enc(layer_rows)
    memory_grad, queried, cross_kept, factors_got, enc_home, layer_rows = stage(
        memory_grad, queried, cross_kept, factors_got, enc_home, layer_rows
    )
    factors = [
        lax.all_gather(
            jnp.where(is_enc, g[: g.shape[0] // 2], got), everyone, axis=0, tiled=True
        )
        for g, got in zip(queried[3], factors_got)
    ]

    def cross_late():
        grad_cross, grad_cross_bf, cmixed, grad_cq, grad_ckv = cross_kept
        grads = jnp.concatenate(
            [
                mm_lt(first_bf, grad_cq).astype(BF),
                mm_lt(memory_low, grad_ckv).astype(BF),
                mm_lt(cmixed, grad_cross_bf).astype(BF),
            ],
            axis=1,
        )
        return grads, grad_cross + mm_rt(grad_cq, cross_full[:, :width])

    cross_grads, dec_first = lax.cond(
        is_enc,
        lambda: (jnp.zeros((width, 4 * width), BF), jnp.zeros((total, width), F32)),
        cross_late,
    )
    scored, q_grad_rows, grad_heat, query_grads, query_small_grads = queried

    def enc_back():
        grad_f, grad_h, grad_first, gain_two, shift_two = feed_back(
            memory_grad.astype(F32), enc_slope, enc_kept
        )
        return grad_f, grad_h, grad_first, (gain_two, shift_two)

    grad_f, grad_h, grad_first, norm_two = lax.cond(
        is_enc, enc_back, lambda: (dec_f, dec_h, dec_first, dec_norm)
    )

    grad_h, grad_f, grad_first, layer_rows = stage(grad_h, grad_f, grad_first, layer_rows)
    dec_home = links.home_dec(layer_rows)
    up_got = links.reduce_open(feed_in, grad_h)
    down_got = links.reduce_open(active, grad_f)
    cross_pair = cross_grads.reshape(2, width // 2, 4 * width)
    cross_got = links.flip(
        lax.dynamic_index_in_dim(cross_pair, 1 - core, 0, keepdims=False), "dec"
    )
    grad_one, gain_one, shift_one = norm_bwd(grad_first, kept_one, gains[0])
    grad_one_bf = grad_one.astype(BF)
    grad_mixed = mm_rt(grad_one_bf, w_out).astype(BF)
    up_got, down_got, cross_got, grad_mixed, dec_home = stage(
        up_got, down_got, cross_got, grad_mixed, dec_home
    )
    cross_sum = lax.dynamic_index_in_dim(cross_pair, core, 0, keepdims=False)
    cross_sum = (cross_sum.astype(F32) + cross_got.astype(F32)).astype(BF)
    cross_sum = cross_sum.reshape((2,) + (2,) * links.bits + (cross_rows, 4 * width))
    up_sum = links.reduce_own(feed_in, grad_h, up_got)
    down_sum = links.reduce_own(active, grad_f, down_got)

    def feed_steps(step):
        return [
            (up_sum, 1, step, "both", 0),
            (down_sum, 2, step, "both", 0),
            (cross_sum, 0, step, "dec", 1),
        ]

    up_sum, down_sum, cross_sum = links.reduce_steps(feed_steps(0))
    grad_joint = attend_back(
        joint, joint, joint, self_off, width, labels, causal, grad_mixed, True
    )
    up_sum, down_sum, cross_sum, grad_joint = stage(up_sum, down_sum, cross_sum, grad_joint)
    split_joint = [(0, joint_w // 2), (joint_w // 2, joint_w)]
    attn_jobs = [(stream_bf, grad_joint[:, a:b]) for a, b in split_joint]
    attn_jobs += [(mixed, grad_one_bf)]
    attn_got = [links.reduce_open(left, right) for left, right in attn_jobs]
    grad_rows = (grad_one + mm_rt(grad_joint, w_joint)).astype(BF)
    up_sum, down_sum, cross_sum = links.reduce_steps(feed_steps(1))

    def role_rows(vec):
        return vec.reshape(n, -1)

    def role_pair_rows(one, two):
        return jnp.stack([role_rows(one), role_rows(two)], axis=1).reshape(n, -1)

    def side_rows(vec):
        lead = vec.reshape(-1, vec.shape[-1]).shape[0]
        return vec.reshape(lead, 2 * n, -1).transpose(1, 0, 2).reshape(2 * n, -1)

    joint_cols = colsum(grad_joint)
    role_grads = jnp.concatenate(
        [
            role_rows(jnp.concatenate([joint_cols[:width], joint_cols[2 * width :]])),
            role_rows(colsum(grad_one_bf)),
            role_rows(colsum(grad_h)),
            role_rows(colsum(grad_f)),
            role_pair_rows(gain_one, norm_two[0]),
            role_pair_rows(shift_one, norm_two[1]),
        ],
        axis=-1,
    )
    def lead_rows(table):
        table = table.reshape(2, 2, half, -1).transpose(0, 2, 1, 3)
        return table.reshape(2, half, -1)

    cross_table = jnp.concatenate([side_rows(v) for v in cross_small_grads], axis=1)
    query_table = jnp.concatenate([side_rows(v) for v in query_small_grads], axis=1)
    small_grads = jnp.concatenate(
        [
            role_grads.reshape(2, half, n_role),
            lead_rows(cross_table),
            lead_rows(query_table),
            jnp.broadcast_to(grad_heat, (2, half, 1)),
        ],
        axis=2,
    )
    small_sum = lax.dynamic_index_in_dim(small_grads, core, 0, keepdims=False)
    small_got = links.flip(lax.dynamic_index_in_dim(small_grads, 1 - core, 0, keepdims=False))
    small_sum = (small_sum + small_got).reshape((2,) * links.bits + (1, -1))
    up_sum, down_sum, cross_sum, attn_got, grad_rows, small_sum = stage(
        up_sum, down_sum, cross_sum, attn_got, grad_rows, small_sum
    )
    rows_home = links.swap(grad_rows)
    for step in range(2, links.bits):
        up_sum = links.reduce_step(up_sum, 1, step)
        down_sum = links.reduce_step(down_sum, 2, step)
        cross_sum = links.reduce_step(cross_sum, 0, step, "dec", 1)
    attn_sum = [
        links.reduce_step(links.reduce_own(left, right, got), turn, 0)
        for turn, ((left, right), got) in enumerate(zip(attn_jobs, attn_got))
    ]
    small_sum = links.reduce_step(small_sum, 0, 0)
    per_block = inquiry_vectors.shape[1]
    score_row = jnp.pad(scored.reshape(1, -1), ((0, 0), (0, q_width - scored.size))).astype(BF)
    q_packet = jnp.concatenate([q_grad_rows.astype(BF), score_row])
    attn_sum, up_sum, down_sum, rows_home, small_sum, cross_sum, factors, q_packet = stage(
        attn_sum, up_sum, down_sum, rows_home, small_sum, cross_sum, factors, q_packet
    )
    up_own = links.swap(up_sum.reshape(-1, ff)).astype(F32)
    down_own = links.swap(down_sum.reshape(-1, width)).astype(F32)
    for step in range(1, links.bits):
        attn_sum = [links.reduce_step(v, turn, step) for turn, v in enumerate(attn_sum)]
        small_sum = links.reduce_step(small_sum, 0, step)
        if step + 1 < links.bits:
            attn_sum, small_sum, factors = stage(attn_sum, small_sum, factors)
    device = core * n + links.dp

    def own_columns(matrix, count):
        wide = matrix.shape[1]
        lines = lax.broadcasted_iota(jnp.int32, (wide, count), 0)
        places = lax.broadcasted_iota(jnp.int32, (wide, count), 1) + device * count
        return mm(matrix, (lines == places).astype(BF)).astype(BF)

    sizes, at, cols = [q_width] * 5 + [q_ff, q_ff] + [q_width] * 3, 0, []
    for size in sizes:
        cols.append(factors[0][:, at : at + size])
        at += size
    f_head, f_q, f_mixed, f_one, f_middle, f_hidden, f_active, f_two, f_asks, f_gmix = cols

    table = factors[1]
    all_asked, all_seen = factors[0].shape[0], table.shape[0]
    lines = lax.broadcasted_iota(jnp.int32, (all_seen, all_asked), 0) // QHEADS
    spread = (lines == lax.broadcasted_iota(jnp.int32, (all_seen, all_asked), 1)).astype(BF)
    row_head = lax.broadcasted_iota(jnp.int32, (all_seen, q_width), 0) % QHEADS
    col_head = lax.broadcasted_iota(jnp.int32, (all_seen, q_width), 1) // (q_width // QHEADS)

    def by_head(seen, other):
        wide = jnp.where(row_head == col_head, mm(spread, other), 0.0).astype(BF)
        return mm_lt(own_columns(seen, q_rows), wide)

    query_k_own = by_head(table[:, :q_width], f_asks) * (q_width // QHEADS) ** (-0.5)
    query_v_own = by_head(table[:, q_width:], f_gmix)
    query_q_own = mm_lt(own_columns(f_head, q_rows), f_q)
    query_out_own = mm_lt(own_columns(f_mixed, q_rows), f_one)
    query_up_own = mm_lt(own_columns(f_middle, q_rows), f_hidden)
    query_down_own = mm_lt(own_columns(f_active, q_rows * q_folds), f_two)
    query_own_mats = [
        jnp.concatenate([query_q_own, query_k_own, query_v_own], axis=1),
        query_out_own,
        query_up_own,
        query_down_own,
    ]
    attn_home = jnp.concatenate([v.reshape(-1, v.shape[-1]) for v in attn_sum], axis=1)
    attn_home = links.swap(attn_home).astype(F32)
    joint_own, out_own = attn_home[:, :joint_w], attn_home[:, joint_w:]
    cross_sum = cross_sum.reshape(2, cross_rows, 4 * width)
    cross_sum = jnp.where(is_enc, links.to_enc(cross_sum[0]), cross_sum[1]).astype(F32)
    cross_own_mats = [
        cross_sum[:, :width],
        cross_sum[:, width : 3 * width],
        cross_sum[:, 3 * width :],
    ]
    small_sum = small_sum.reshape(-1)
    role_own = links.swap(small_sum[:n_role])
    cross_pair = small_sum[n_role : n_role + 2 * n_cross].reshape(2, n_cross)
    query_pair = small_sum[n_role + 2 * n_cross : n_role + 2 * n_cross + 2 * n_query]
    pairs = jnp.concatenate([cross_pair, query_pair.reshape(2, n_query)], axis=1)
    keep_side = jnp.concatenate([jnp.where(is_enc, pairs[0], pairs[1]), small_sum[-1:]])
    send_side = jnp.concatenate([jnp.where(is_enc, pairs[1], pairs[0]), small_sum[-1:]])
    side_own = keep_side + links.across(send_side)
    cross_own = side_own[:n_cross]
    query_own = side_own[n_cross : n_cross + n_query]
    heat_total = side_own[-1:]

    layer_out = jnp.where(core == 0, enc_home, dec_home).reshape(1, micro, rows, width)
    input_grad = rows_home.astype(F32).reshape(1, micro, rows, width)

    q_home = links.home_enc(q_packet)
    q_mats = q_home[: micro * per_block].reshape(micro, per_block, q_width)
    s_mats = q_home[micro * per_block :, : scored.size].reshape(micro, 1, -1)
    second = jnp.concatenate(
        [q_mats[1], jnp.pad(s_mats[1], ((0, 0), (0, q_width - s_mats.shape[2])))]
    )
    got_second = lax.ppermute(second, "phase", [(0, 1)])
    question_grad = jnp.where(core == 0, q_mats[0], got_second[:per_block]).astype(F32)[None]
    own_scores = jnp.where(core == 0, s_mats[0], got_second[per_block:, : s_mats.shape[2]])
    scores = own_scores.astype(F32).reshape(1, asked, chosen_count)

    sizes = [
        intrinsic_probe_content_offset.shape[1],
        intrinsic_mixing_result_offset.shape[1],
        perceptron_widen_offset.shape[1],
        perceptron_narrow_offset.shape[1],
        2 * standardize_scales.shape[2],
        2 * standardize_shifts.shape[2],
    ]
    cut, role_out = 0, []
    for size in sizes:
        role_out.append(role_own[cut : cut + size])
        cut += size
    role_tuple = (
        joint_own[None],
        role_out[0][None],
        out_own[None],
        role_out[1][None],
        up_own[None],
        role_out[2][None],
        down_own[None],
        role_out[3][None],
        role_out[4].reshape(1, 2, -1),
        role_out[5].reshape(1, 2, -1),
    )
    c = cross_own.reshape(5, -1)
    cross_tuple = (
        cross_own_mats[0],
        c[0],
        cross_own_mats[1],
        c[1],
        cross_own_mats[2],
        c[2],
        c[3],
        c[4],
    )
    cut, q_out = 0, []
    for part in (
        retriever_probe_content_offset,
        retriever_mixing_result_offset,
        retriever_widen_offset,
        retriever_narrow_offset,
        retriever_standardize_scales,
        retriever_standardize_shifts,
    ):
        q_out.append(query_own[cut : cut + part.size].reshape(part.shape))
        cut += part.size
    query_tuple = (
        query_own_mats[0],
        q_out[0],
        query_own_mats[1],
        q_out[1],
        query_own_mats[2],
        q_out[2],
        query_own_mats[3],
        q_out[3],
        q_out[4],
        q_out[5],
    )
    return (
        (layer_out, input_grad, scores, question_grad, heat_total)
        + role_tuple
        + cross_tuple
        + query_tuple
    )


def solution(mesh):
    row = P(None, "dp", None)
    mat, vec = P("phase", "dp", None), P("phase", "dp")
    pair = P("phase", None, "dp")
    side_mat, side_vec = P(("phase", "dp"), None), P(("phase", "dp"))
    side_pair = P(None, ("phase", "dp"))
    role = (mat, vec, mat, vec, mat, vec, mat, vec, pair, pair)
    cross = (side_mat, side_vec, side_mat, side_vec, side_mat, side_vec, side_vec, side_vec)
    query = (side_mat, side_vec) * 4 + (side_pair, side_pair)
    stream = P("phase", None, "dp", None)
    in_specs = (stream,) + (row,) * 7 + (P(),) + role + cross + query
    out_specs = (stream, stream, mat, mat, P()) + role + cross + query
    return jax.shard_map(local, mesh=mesh, in_specs=in_specs, out_specs=out_specs, check_vma=False)
```

```python
from functools import partial

import jax
import jax.numpy as jnp
from jax import lax
from jax.experimental import pallas as pl
from jax.experimental.pallas import tpu as pltpu
from jax.sharding import PartitionSpec as P

HEADS = 16
QHEADS = 12
NEG_FILL = -1e30
EPS_MODEL = 1e-05
EPS_QUERY = 1e-12
BF = jnp.bfloat16
F32 = jnp.float32


def mm(left, right):
    return jnp.dot(left, right, preferred_element_type=F32)


def mm_lt(left, right):
    return lax.dot_general(left, right, (((0,), (0,)), ((), ())), preferred_element_type=F32)


def mm_rt(left, right):
    return lax.dot_general(left, right, (((1,), (1,)), ((), ())), preferred_element_type=F32)


def colsum(matrix):
    return jnp.sum(matrix.astype(F32), axis=0)


def norm_fwd(stream, gain, bias, eps):
    centred = stream - jnp.mean(stream, axis=-1, keepdims=True)
    rstd = lax.rsqrt(jnp.mean(centred * centred, axis=-1, keepdims=True) + eps)
    hat = centred * rstd
    return hat * gain + bias, (hat, rstd)


def norm_bwd(grad, kept, gain):
    hat, rstd = kept
    scaled = grad * gain
    centre = jnp.mean(scaled, axis=-1, keepdims=True)
    along = jnp.mean(scaled * hat, axis=-1, keepdims=True)
    return rstd * (scaled - centre - hat * along), jnp.sum(grad * hat, axis=0), jnp.sum(grad, axis=0)


def gelu_pair(hidden):
    cdf = 0.5 * (1.0 + lax.erf(hidden * 0.7071067811865476))
    pdf = jnp.exp(-0.5 * hidden * hidden) * 0.3989422804014327
    return (hidden * cdf).astype(BF), (cdf + hidden * pdf).astype(BF)


def allowed_bias(key_ref, query_ref, causal_ref):
    same = key_ref[0] == query_ref[0]
    keys = lax.broadcasted_iota(jnp.int32, same.shape, 0)
    queries = lax.broadcasted_iota(jnp.int32, same.shape, 1)
    seen = jnp.logical_and(same, jnp.logical_or(queries >= keys, causal_ref[0] == 0))
    return jnp.where(seen, 0.0, NEG_FILL).astype(F32)


def attn_fwd_body(
    head_size, q_off, k_off, v_off, causal_ref, key_ref, query_ref, q_ref, k_ref, v_ref, o_ref
):
    bias = allowed_bias(key_ref, query_ref, causal_ref)
    scale = head_size ** (-0.5)
    pairs = o_ref.shape[1] // 128

    def one(pair, carry):
        at = pl.multiple_of(pair * 128, 128)
        q2 = q_ref[:, pl.ds(q_off + at, 128)]
        q2 = (q2.astype(F32) * scale).astype(BF)
        k2 = k_ref[:, pl.ds(k_off + at, 128)]
        v_t = v_ref[:, pl.ds(v_off + at, 128)].T
        lane = lax.broadcasted_iota(jnp.int32, q2.shape, 1) < head_size
        mixed = []
        for mine in (lane, jnp.logical_not(lane)):
            scores = mm_rt(k2, jnp.where(mine, q2, jnp.zeros_like(q2))) + bias
            raised = jnp.exp(scores - jnp.max(scores, axis=0, keepdims=True))
            total = jnp.sum(raised, axis=0, keepdims=True)
            mixed.append(mm(v_t, raised.astype(BF)) * (1.0 / total))
        row = lax.broadcasted_iota(jnp.int32, mixed[0].shape, 0) < head_size
        o_ref[:, pl.ds(at, 128)] = jnp.where(row, mixed[0], mixed[1]).T.astype(BF)
        return carry

    lax.fori_loop(0, pairs, one, 0)


def attn_bwd_body(
    head_size, q_off, k_off, v_off, joint, causal_ref, key_ref, query_ref, q_ref, k_ref, v_ref, g_ref, *outs
):
    bias = allowed_bias(key_ref, query_ref, causal_ref)
    scale = head_size ** (-0.5)
    pairs = g_ref.shape[1] // 128
    dq_ref, dk_ref, dv_ref = (outs[0],) * 3 if joint else (outs[0], outs[1], outs[1])

    def one(pair, carry):
        at = pl.multiple_of(pair * 128, 128)
        q2 = q_ref[:, pl.ds(q_off + at, 128)]
        q2 = (q2.astype(F32) * scale).astype(BF)
        k2 = k_ref[:, pl.ds(k_off + at, 128)]
        v2 = v_ref[:, pl.ds(v_off + at, 128)]
        g2 = g_ref[:, pl.ds(at, 128)]
        k_t = k2.T
        lane = lax.broadcasted_iota(jnp.int32, q2.shape, 1) < head_size
        parts = []
        for mine in (lane, jnp.logical_not(lane)):
            scores = mm_rt(k2, jnp.where(mine, q2, jnp.zeros_like(q2))) + bias
            raised = jnp.exp(scores - jnp.max(scores, axis=0, keepdims=True))
            chances = raised * (1.0 / jnp.sum(raised, axis=0, keepdims=True))
            grad_p = mm_rt(v2, jnp.where(mine, g2, jnp.zeros_like(g2)))
            inner = jnp.sum(chances * grad_p, axis=0, keepdims=True)
            grad_s = (chances * (grad_p - inner)).astype(BF)
            grad_v = mm(chances.astype(BF), g2)
            grad_k = mm(grad_s, q2)
            grad_q_t = mm(k_t, grad_s)
            parts.append((grad_q_t, grad_k, grad_v))
        row = lax.broadcasted_iota(jnp.int32, parts[0][0].shape, 0) < head_size
        grad_q = jnp.where(row, parts[0][0], parts[1][0]).T * scale
        dq_ref[:, pl.ds(q_off + at, 128)] = grad_q.astype(BF)
        dk_ref[:, pl.ds(k_off + at, 128)] = jnp.where(lane, parts[0][1], parts[1][1]).astype(BF)
        dv_ref[:, pl.ds(v_off + at, 128)] = jnp.where(lane, parts[0][2], parts[1][2]).astype(BF)
        return carry

    lax.fori_loop(0, pairs, one, 0)


def attn_specs(rows, arrays):
    specs = [
        pl.BlockSpec(memory_space=pltpu.SMEM),
        pl.BlockSpec((1, rows, 1), lambda m: (m, 0, 0)),
        pl.BlockSpec((1, 1, rows), lambda m: (m, 0, 0)),
    ]
    return specs + [pl.BlockSpec((rows, a.shape[1]), lambda m: (m, 0)) for a in arrays]


def attn_params():
    return pltpu.CompilerParams(dimension_semantics=("arbitrary",), vmem_limit_bytes=48 << 20)


def attn_cost(total, rows, width, products):
    return pl.CostEstimate(
        flops=2 * products * total * rows * width,
        transcendentals=total * rows * HEADS,
        bytes_accessed=total * width * 2 * (4 if products == 2 else 7),
    )


def attend(q, k, v, offsets, width, labels, causal):
    rows = labels.shape[1]
    total = q.shape[0]
    return pl.pallas_call(
        partial(attn_fwd_body, width // HEADS, *offsets),
        grid=(total // rows,),
        in_specs=attn_specs(rows, (q, k, v)),
        out_specs=pl.BlockSpec((rows, width), lambda m: (m, 0)),
        out_shape=jax.ShapeDtypeStruct((total, width), BF),
        compiler_params=attn_params(),
        cost_estimate=attn_cost(total, rows, width, 2),
        name="attend_fwd",
    )(causal, labels[:, :, None], labels[:, None, :], q, k, v)


def attend_back(q, k, v, offsets, width, labels, causal, grad, joint):
    rows = labels.shape[1]
    total = q.shape[0]
    widths = (3 * width,) if joint else (width, 2 * width)
    out = pl.pallas_call(
        partial(attn_bwd_body, width // HEADS, *offsets, joint),
        grid=(total // rows,),
        in_specs=attn_specs(rows, (q, k, v, grad)),
        out_specs=[pl.BlockSpec((rows, w), lambda m: (m, 0)) for w in widths],
        out_shape=[jax.ShapeDtypeStruct((total, w), BF) for w in widths],
        compiler_params=attn_params(),
        cost_estimate=attn_cost(total, rows, width, 5),
        name="attend_bwd",
    )(causal, labels[:, :, None], labels[:, None, :], q, k, v, grad)
    return out[0] if joint else tuple(out)


def heads_of(matrix, count):
    return matrix.reshape(matrix.shape[0], count, matrix.shape[1] // count)


def query_work(
    rows_bf, firsts, ends, chosen, adjoint, heat, sheet, hidden_size, shards, vectors
):
    b_joint, b_out, b_up, b_down, gains, shifts = vectors
    width = rows_bf.shape[1]
    folds = hidden_size // width
    w_joint = sheet[:, : 3 * width]
    w_out = sheet[:, 3 * width : 4 * width]
    w_up = sheet[:, 4 * width : 4 * width + hidden_size]
    downs = [
        sheet[:, 4 * width + hidden_size + i * width : 5 * width + hidden_size + i * width]
        for i in range(folds)
    ]

    def fold(matrix):
        split = matrix.reshape(matrix.shape[0], shards, folds, -1)
        return [split[:, :, i].reshape(matrix.shape[0], width) for i in range(folds)]

    def unfold(parts):
        split = [p.reshape(p.shape[0], shards, 1, -1) for p in parts]
        return jnp.concatenate(split, axis=2).reshape(parts[0].shape[0], -1)

    scale = (width // QHEADS) ** (-0.5)
    positions = jnp.arange(rows_bf.shape[0], dtype=jnp.int32)
    allowed = (positions[None, :] >= firsts[:, None]) & (positions[None, :] < ends[:, None])
    pick = (positions[None, :] == firsts[:, None]).astype(BF)
    head_bf = mm(pick, rows_bf).astype(BF)
    queries = (mm(head_bf, w_joint[:, :width]) + b_joint[:width]).astype(BF)
    paired = mm(rows_bf, w_joint[:, width:])
    keys = paired[:, :width].astype(BF)
    values = (paired[:, width:] + b_joint[width:]).astype(BF)
    qh, kh, vh = heads_of(queries, QHEADS), heads_of(keys, QHEADS), heads_of(values, QHEADS)
    scores = jnp.einsum("qhd,khd->hqk", qh, kh, preferred_element_type=F32) * scale
    scores = jnp.where(allowed[None], scores, NEG_FILL)
    chances = jax.nn.softmax(scores, axis=-1)
    chances_bf = chances.astype(BF)
    mixed = jnp.einsum("hqk,khd->qhd", chances_bf, vh, preferred_element_type=F32)
    mixed = mixed.reshape(queries.shape).astype(BF)
    branch = mm(mixed, w_out) + b_out
    middle, kept_one = norm_fwd(head_bf.astype(F32) + branch, gains[0], shifts[0], EPS_QUERY)
    middle_bf = middle.astype(BF)
    active, slope = gelu_pair(mm(middle_bf, w_up) + b_up)
    folded = fold(active)
    fed = sum(mm(part, down) for part, down in zip(folded, downs))
    found, kept_two = norm_fwd(middle + fed + b_down, gains[1], shifts[1], EPS_QUERY)
    raw = jnp.sum(found[:, None, :] * chosen, axis=-1)
    scored = raw / heat
    grad_heat = -jnp.sum(adjoint * raw) / (heat * heat)
    grad_found = jnp.sum((adjoint / heat)[:, :, None] * chosen, axis=1)
    grad_two, gain_two, shift_two = norm_bwd(grad_found, kept_two, gains[1])
    grad_two_bf = grad_two.astype(BF)
    grad_active = unfold([mm_rt(grad_two_bf, down) for down in downs])
    grad_hidden = (grad_active * slope.astype(F32)).astype(BF)
    grad_middle = grad_two + mm_rt(grad_hidden, w_up)
    grad_one, gain_one, shift_one = norm_bwd(grad_middle, kept_one, gains[0])
    grad_one_bf = grad_one.astype(BF)
    grad_mixed = heads_of(mm_rt(grad_one_bf, w_out).astype(BF), QHEADS)
    grad_values = jnp.einsum("hqk,qhd->khd", chances_bf, grad_mixed, preferred_element_type=F32)
    grad_chances = jnp.einsum("qhd,khd->hqk", grad_mixed, vh, preferred_element_type=F32)
    inner = jnp.sum(chances * grad_chances, axis=-1, keepdims=True)
    grad_scores = (chances * (grad_chances - inner)).astype(BF)
    grad_q = jnp.einsum("hqk,khd->qhd", grad_scores, kh, preferred_element_type=F32) * scale
    grad_k = jnp.einsum("hqk,qhd->khd", grad_scores, qh, preferred_element_type=F32) * scale
    grad_q = grad_q.reshape(queries.shape).astype(BF)
    grad_kv = jnp.concatenate(
        [grad_k.reshape(keys.shape), grad_values.reshape(keys.shape)], axis=1
    ).astype(BF)
    grad_heads = grad_one + mm_rt(grad_q, w_joint[:, :width])
    spread = lax.dot_general(
        pick.astype(F32), grad_heads, (((0,), (0,)), ((), ())),
        precision=lax.Precision.HIGHEST, preferred_element_type=F32,
    )
    grad_rows = mm_rt(grad_kv, w_joint[:, width:]) + spread
    factors = [
        head_bf, grad_q, mixed, grad_one_bf, middle_bf, grad_hidden, active, grad_two_bf,
        queries, grad_mixed.reshape(queries.shape),
    ]
    seen = [
        jnp.einsum("hqk,kd->qhd", p, rows_bf, preferred_element_type=F32)
        for p in (grad_scores, chances_bf)
    ]
    seen = jnp.concatenate(seen, axis=2).astype(BF).reshape(-1, 2 * width)
    mats = (jnp.concatenate(factors, axis=1), seen)
    smalls = (
        jnp.concatenate([colsum(grad_q), colsum(grad_kv[:, width:])]),
        colsum(grad_one_bf),
        colsum(grad_hidden),
        colsum(grad_two_bf),
        jnp.stack([gain_one, gain_two]),
        jnp.stack([shift_one, shift_two]),
    )
    return scored, grad_rows, grad_heat, mats, smalls


class Links:
    def __init__(self):
        self.n = lax.axis_size("dp")
        self.half = self.n // 2
        self.bits = self.half.bit_length() - 1
        self.core = lax.axis_index("phase")
        self.dp = lax.axis_index("dp")
        self.is_enc = self.dp < self.half

    def all_pairs(self, value, pairs):
        return lax.ppermute(value, ("phase", "dp"), pairs)

    def swap(self, value):
        n, h = self.n, self.half
        pairs = []
        for i in range(h):
            pairs += [(i, i), (n + i, i + h), (i + h, n + i), (n + i + h, n + i + h)]
        return self.all_pairs(value, pairs)

    def pull_enc(self, value):
        n, h = self.n, self.half
        pairs = []
        for i in range(h):
            pairs += [(i, i), (i + h, n + i)]
        return self.all_pairs(value, pairs)

    def home_enc(self, value):
        n, h = self.n, self.half
        pairs = []
        for i in range(h):
            pairs += [(i, i), (n + i, i + h)]
        return self.all_pairs(value, pairs)

    def home_dec(self, value):
        n, h = self.n, self.half
        pairs = []
        for i in range(h):
            pairs += [(n + i + h, n + i + h), (i + h, n + i)]
        return self.all_pairs(value, pairs)

    def push_dec(self, value):
        n, h = self.n, self.half
        pairs = []
        for i in range(h):
            pairs += [(n + i + h, n + i + h), (n + i, i + h)]
        return self.all_pairs(value, pairs)

    def to_dec(self, value):
        return lax.ppermute(value, "dp", [(i, i + self.half) for i in range(self.half)])

    def to_enc(self, value):
        return lax.ppermute(value, "dp", [(i + self.half, i) for i in range(self.half)])

    def across(self, value):
        h = self.half
        pairs = [(i, i + h) for i in range(h)] + [(i + h, i) for i in range(h)]
        return lax.ppermute(value, "dp", pairs)

    def flip(self, value, who="both"):
        first = self.half if who == "dec" else 0
        last = self.half if who == "enc" else self.n
        pairs = []
        for i in range(first, last):
            pairs += [(i, self.n + i), (self.n + i, i)]
        return self.all_pairs(value, pairs)

    def hop(self, value, bit, who):
        first = self.half if who == "dec" else 0
        last = self.half if who == "enc" else self.n
        return lax.ppermute(value, "dp", [(i, i ^ (1 << bit)) for i in range(first, last)])

    def order(self, turn):
        return [(turn + k) % self.bits for k in range(self.bits)]

    def gather_hop(self, held, turn, step, who="both"):
        return self.hop(held, self.order(turn)[step], who)

    def places(self, turn, lead=1):
        order = self.order(turn)
        mine = self.dp % self.half
        masks = [
            sum(((p >> j) & 1) << order[j] for j in range(self.bits)) for p in range(self.half)
        ]
        own = jnp.stack(
            [jnp.bitwise_xor(mine, m) + r * self.half for m in masks for r in range(lead)]
        ).astype(jnp.int32)
        wide = lead * self.half
        return jnp.concatenate([own + self.core * wide, own + (1 - self.core) * wide])

    def half_of(self, left, core):
        wide = left.shape[1] // 2
        return lax.dynamic_slice_in_dim(left, core * wide, wide, 1)

    def reduce_open(self, left, right):
        return self.flip(mm_lt(self.half_of(left, 1 - self.core), right).astype(BF))

    def reduce_own(self, left, right, got):
        own = mm_lt(self.half_of(left, self.core), right) + got.astype(F32)
        shard = left.shape[1] // self.n
        return own.astype(BF).reshape((2,) * self.bits + (shard, right.shape[1]))

    def reduce_steps(self, jobs):
        keeps, gots = [], []
        for value, turn, step, who, lead in jobs:
            bit = self.order(turn)[step]
            mine = (self.dp >> bit) & 1
            axis = lead + self.bits - 1 - bit
            send = lax.dynamic_slice_in_dim(value, 1 - mine, 1, axis)
            keeps.append(lax.dynamic_slice_in_dim(value, mine, 1, axis))
            gots.append(self.hop(send, bit, who))
        gots = lax.optimization_barrier(tuple(gots))
        return [
            (keep.astype(F32) + got.astype(F32)).astype(keep.dtype)
            for keep, got in zip(keeps, gots)
        ]

    def reduce_step(self, value, turn, step, who="both", lead=0):
        bit = self.order(turn)[step]
        mine = (self.dp >> bit) & 1
        axis = lead + self.bits - 1 - bit
        send = lax.dynamic_slice_in_dim(value, 1 - mine, 1, axis)
        keep = lax.dynamic_slice_in_dim(value, mine, 1, axis)
        got = self.hop(send, bit, who)
        return (keep.astype(F32) + got.astype(F32)).astype(value.dtype)


def weave_body(quarter, streams, place_ref, *refs):
    count = len(streams)
    at = pl.program_id(0)
    for index in range(4):

        @pl.when(jnp.logical_and(at >= index * quarter, at < (index + 1) * quarter))
        def _(index=index):
            out = 4 * count
            for stream, widths in enumerate(streams):
                low = 0
                for width in widths:
                    refs[out][...] = refs[4 * stream + index][0, :, low : low + width]
                    low += width
                    out += 1


def weave(streams, places, widths):
    quarter = streams[0][0].shape[0]
    total = 4 * quarter

    def source(part, index):
        return pl.BlockSpec(
            (1,) + part.shape[1:],
            lambda g, place: (jnp.clip(g - index * quarter, 0, quarter - 1), 0, 0),
        )

    def target(rows, width, stream):
        return pl.BlockSpec((rows, width), lambda g, place: (place[stream, g], 0))

    shapes = [
        (parts[0].shape[1], w, i)
        for i, (parts, ws) in enumerate(zip(streams, widths))
        for w in ws
    ]
    moved = sum(4 * p.size for parts in streams for p in parts)
    return pl.pallas_call(
        partial(weave_body, quarter, widths),
        grid_spec=pltpu.PrefetchScalarGridSpec(
            num_scalar_prefetch=1,
            grid=(total,),
            in_specs=[source(p, i) for parts in streams for i, p in enumerate(parts)],
            out_specs=[target(*shape) for shape in shapes],
        ),
        out_shape=[jax.ShapeDtypeStruct((total * r, w), BF) for r, w, _ in shapes],
        compiler_params=pltpu.CompilerParams(
            dimension_semantics=("arbitrary",), vmem_limit_bytes=48 << 20
        ),
        cost_estimate=pl.CostEstimate(flops=0, transcendentals=0, bytes_accessed=moved),
        name="weave",
    )(places, *[p for parts in streams for p in parts])


def stage(*values):
    return lax.optimization_barrier(values)


def block_of(values, rows):
    flat = jnp.concatenate([v.reshape(1, -1).astype(BF) for v in values], axis=1)
    return jnp.pad(flat, ((0, 0), (0, rows * 128 - flat.size))).reshape(rows, 128)


def local(
    token_vectors,
    generation_result_adjoint,
    sequence_labels,
    inquiry_vectors,
    inquiry_token_spans,
    document_vectors,
    document_slots,
    relevance_adjoint,
    softness_scalar,
    intrinsic_triple_map,
    intrinsic_probe_content_offset,
    intrinsic_mixing_result_map,
    intrinsic_mixing_result_offset,
    perceptron_widen_map,
    perceptron_widen_offset,
    perceptron_narrow_map,
    perceptron_narrow_offset,
    standardize_scales,
    standardize_shifts,
    encoded_mixing_probe_map,
    encoded_mixing_probe_offset,
    encoded_lookup_content_map,
    encoded_mixing_content_offset,
    encoded_mixing_result_map,
    encoded_mixing_result_offset,
    encoded_mixing_scale_factor,
    encoded_mixing_scale_shift,
    retriever_triple_map,
    retriever_probe_content_offset,
    retriever_mixing_result_map,
    retriever_mixing_result_offset,
    retriever_widen_map,
    retriever_widen_offset,
    retriever_narrow_map,
    retriever_narrow_offset,
    retriever_standardize_scales,
    retriever_standardize_shifts,
):
    links = Links()
    n, half, is_enc, core = links.n, links.half, links.is_enc, links.core
    micro, rows, width = token_vectors.shape[1:]
    total = micro * rows
    joint_w = intrinsic_triple_map.shape[2]
    ff = perceptron_widen_map.shape[2]
    heat = softness_scalar[0]

    role_vecs = (
        intrinsic_probe_content_offset,
        intrinsic_mixing_result_offset,
        perceptron_widen_offset,
        perceptron_narrow_offset,
        standardize_scales,
        standardize_shifts,
    )
    cross_vecs = (
        encoded_mixing_probe_offset,
        encoded_mixing_content_offset,
        encoded_mixing_result_offset,
        encoded_mixing_scale_factor,
        encoded_mixing_scale_shift,
    )
    query_vecs = (
        retriever_probe_content_offset,
        retriever_mixing_result_offset,
        retriever_widen_offset,
        retriever_narrow_offset,
        retriever_standardize_scales,
        retriever_standardize_shifts,
    )
    n_role = sum(v.size for v in role_vecs)
    n_cross = sum(v.size for v in cross_vecs)
    n_query = sum(v.size for v in query_vecs)
    everyone = ("phase", "dp")
    shard_rows = intrinsic_triple_map.shape[1]
    q_width = inquiry_vectors.shape[2]
    q_ff = retriever_widen_map.shape[1]
    q_rows = retriever_triple_map.shape[0]
    q_folds = q_ff // q_width
    cross_rows = encoded_mixing_probe_map.shape[0]

    def vectors_of(table, like):
        at, out = 0, []
        for vec in like:
            lead = vec.shape[-2] if vec.ndim > 1 and vec.shape[-2] > 1 else 1
            piece = table[:, at : at + vec.size].reshape(table.shape[0], lead, -1)
            piece = piece.transpose(1, 0, 2).reshape(lead, -1)
            out.append(piece if lead > 1 else piece[0])
            at += vec.size
        return out

    attn_in = jnp.concatenate(
        [
            intrinsic_triple_map[0],
            intrinsic_mixing_result_map[0],
            block_of(role_vecs + (sequence_labels,), shard_rows),
        ],
        axis=1,
    )
    held = list(
        stage(
            links.swap(attn_in),
            links.swap(perceptron_widen_map[0]),
            links.swap(perceptron_narrow_map[0]),
        )
    )
    labels = held[0][:, joint_w + width :].reshape(1, -1)[:, n_role : n_role + total]
    labels = labels.astype(jnp.int32).reshape(micro, rows)
    held = [v[None] for v in held]
    tokens_in = token_vectors[0].reshape(total, width)
    adjoint_own = generation_result_adjoint.reshape(total, width)
    query_in = jnp.concatenate(
        [retriever_triple_map, retriever_mixing_result_map, retriever_widen_map]
        + [retriever_narrow_map[i * q_rows : (i + 1) * q_rows] for i in range(q_folds)]
        + [block_of(query_vecs, q_rows)],
        axis=1,
    )
    cross_in = jnp.concatenate(
        [
            encoded_mixing_probe_map,
            encoded_lookup_content_map,
            encoded_mixing_result_map,
            block_of(cross_vecs, cross_rows),
        ],
        axis=1,
    )
    asked = inquiry_token_spans.shape[2]
    chosen_count = document_slots.shape[2]
    ints = jnp.concatenate(
        [
            inquiry_token_spans.reshape(1, -1).astype(F32),
            document_slots.reshape(1, -1).astype(F32),
            relevance_adjoint.reshape(1, -1),
        ],
        axis=1,
    )
    doc_own = jnp.concatenate(
        [
            document_vectors.reshape(-1, q_width),
            jnp.pad(ints, ((0, 0), (0, q_width - ints.size))),
        ]
    )
    q_own = inquiry_vectors.reshape(-1, q_width)
    last = links.bits - 1
    cross_full = lax.all_gather(cross_in, everyone, axis=0, tiled=True)
    for step in range(last):
        held = [
            jnp.concatenate([v, links.gather_hop(v, turn, step)], axis=0)
            for turn, v in enumerate(held)
        ]
        if step == 0:
            (held,) = stage(held)
        else:
            held, cross_full = stage(held, cross_full)
    recv = [links.gather_hop(v, turn, last) for turn, v in enumerate(held)]
    theirs = [links.flip(v) for v in held]
    recv, theirs, query_in, tokens_in = stage(recv, theirs, query_in, tokens_in)
    stream_bf = links.swap(tokens_in)
    query_full = lax.all_gather(query_in, everyone, axis=0, tiled=True)
    got = [links.flip(v) for v in recv]
    w_joint, w_out, w_small, w_up, w_down = weave(
        list(zip(held, recv, theirs, got)),
        jnp.stack([links.places(turn) for turn in range(3)]),
        ((joint_w, width, 128), (ff,), (width,)),
    )
    mine_small = w_small.reshape(n, -1)[:, :n_role].astype(F32)
    b_joint, b_out, b_up, b_down, gains, shifts = vectors_of(mine_small, role_vecs)

    causal = jnp.where(is_enc, 0, 1).astype(jnp.int32).reshape(1)
    plain = jnp.zeros((1,), jnp.int32)
    stream = stream_bf.astype(F32)
    bias_joint = jnp.concatenate([b_joint[:width], jnp.zeros((width,), F32), b_joint[width:]])
    joint = (mm(stream_bf, w_joint) + bias_joint).astype(BF)
    self_off = (0, width, 2 * width)
    joint, adjoint_own, doc_own, q_own = stage(joint, adjoint_own, doc_own, q_own)
    adjoint_bf = links.push_dec(adjoint_own)
    doc_packet = links.pull_enc(doc_own)
    q_block_rows = links.pull_enc(q_own)
    mixed = attend(joint, joint, joint, self_off, width, labels, causal)
    first, kept_one = norm_fwd(stream + mm(mixed, w_out) + b_out, gains[0], shifts[0], EPS_MODEL)
    first_bf = first.astype(BF)
    first, first_bf, kept_one, adjoint_bf, doc_packet, q_block_rows = stage(
        first, first_bf, kept_one, adjoint_bf, doc_packet, q_block_rows
    )

    def feed(stream_one, stream_one_bf):
        active, slope = gelu_pair(mm(stream_one_bf, w_up) + b_up)
        result, kept = norm_fwd(
            stream_one + mm(active, w_down) + b_down, gains[1], shifts[1], EPS_MODEL
        )
        return result.astype(BF), active, slope, kept

    def feed_back(grad_result, slope, kept):
        grad_two, gain_two, shift_two = norm_bwd(grad_result, kept, gains[1])
        grad_f = grad_two.astype(BF)
        grad_h = (mm_rt(grad_f, w_down) * slope.astype(F32)).astype(BF)
        return grad_f, grad_h, grad_two + mm_rt(grad_h, w_up), gain_two, shift_two

    def blank(shapes):
        return jax.tree.map(lambda s: jnp.zeros(s.shape, s.dtype), shapes)

    def when(flag, work):
        return lax.cond(flag, work, lambda: blank(jax.eval_shape(work)))

    enc_out, enc_active, enc_slope, enc_kept = when(is_enc, lambda: feed(first, first_bf))
    (enc_out,) = stage(enc_out)
    memory_low = links.to_dec(enc_out)
    (memory_low,) = stage(memory_low)

    cross_off = (0, 0, width)

    def decoder_branch():
        w_cq = cross_full[:, :width]
        w_ckv = cross_full[:, width : 3 * width]
        w_co = cross_full[:, 3 * width : 4 * width]
        cross_small = cross_full[:, 4 * width :]
        cross_small = cross_small.reshape(2 * n, -1).astype(F32)
        cb_q, cb_v, cb_o, c_gain, c_shift = vectors_of(cross_small, cross_vecs)
        cq = (mm(first_bf, w_cq) + cb_q).astype(BF)
        bias_kv = jnp.concatenate([jnp.zeros((width,), F32), cb_v])
        ckv = (mm(memory_low, w_ckv) + bias_kv).astype(BF)
        cmixed = attend(cq, ckv, ckv, cross_off, width, labels, plain)
        second, kept_cross = norm_fwd(
            first + mm(cmixed, w_co) + cb_o, c_gain, c_shift, EPS_MODEL
        )
        second_bf = second.astype(BF)
        decoded, active, slope, kept = feed(second, second_bf)
        grad_f, grad_h, grad_second, gain_two, shift_two = feed_back(
            adjoint_bf.astype(F32), slope, kept
        )
        grad_cross, cgain, cshift = norm_bwd(grad_second, kept_cross, c_gain)
        grad_cross_bf = grad_cross.astype(BF)
        grad_cmixed = mm_rt(grad_cross_bf, w_co).astype(BF)
        grad_cq, grad_ckv = attend_back(
            cq, ckv, ckv, cross_off, width, labels, plain, grad_cmixed, False
        )
        grad_memory = mm_rt(grad_ckv, w_ckv).astype(BF)
        cross_small_grads = (
            colsum(grad_cq),
            colsum(grad_ckv[:, width:]),
            colsum(grad_cross_bf),
            cgain,
            cshift,
        )
        return (
            decoded,
            grad_memory,
            second_bf,
            active,
            grad_f,
            grad_h,
            (gain_two, shift_two),
            cross_small_grads,
            (grad_cross, grad_cross_bf, cmixed, grad_cq, grad_ckv),
        )

    shapes = jax.eval_shape(decoder_branch)
    dec = lax.cond(
        is_enc,
        lambda: (enc_out, jnp.zeros((total, width), BF), first_bf, enc_active) + blank(shapes[4:]),
        decoder_branch,
    )
    (
        layer_rows, grad_memory, feed_in, active, dec_f, dec_h, dec_norm, cross_small_grads, cross_kept
    ) = dec
    grad_memory, cross_kept, query_full, layer_rows = stage(
        grad_memory, cross_kept, query_full, layer_rows
    )

    passages = document_vectors.shape[1]
    n_span, n_pick = micro * asked, micro * asked * chosen_count

    def query_branch():
        tail = doc_packet[micro * passages]
        spans = tail[:n_span].astype(jnp.int32).reshape(micro, asked)
        slots = tail[n_span : n_span + n_pick].astype(jnp.int32).reshape(micro, asked, chosen_count)
        adjoint = tail[n_span + n_pick : n_span + 2 * n_pick].reshape(n_span, chosen_count)
        base = jnp.arange(micro, dtype=jnp.int32)[:, None]
        per_block = inquiry_vectors.shape[1]
        ends = jnp.cumsum(spans, axis=1)
        firsts = (ends - spans + base * per_block).reshape(-1)
        ends = (ends + base * per_block).reshape(-1)
        where_doc = (slots + base[:, :, None] * passages).reshape(n_span, chosen_count)
        query_small = query_full[:, 4 * q_width + 2 * q_ff :].reshape(2 * n, -1).astype(F32)
        return query_work(
            q_block_rows,
            firsts,
            ends,
            doc_packet[where_doc],
            adjoint,
            heat,
            query_full,
            q_ff,
            2 * n,
            vectors_of(query_small, query_vecs),
        )

    queried = when(is_enc, query_branch)
    memory_grad = links.to_enc(grad_memory)
    queried, layer_rows = stage(queried, layer_rows)
    factors_got = [links.to_dec(g[g.shape[0] // 2 :]) for g in queried[3]]
    enc_home = links.home_enc(layer_rows)
    memory_grad, queried, cross_kept, factors_got, enc_home, layer_rows = stage(
        memory_grad, queried, cross_kept, factors_got, enc_home, layer_rows
    )
    factors = [
        lax.all_gather(
            jnp.where(is_enc, g[: g.shape[0] // 2], got), everyone, axis=0, tiled=True
        )
        for g, got in zip(queried[3], factors_got)
    ]

    def cross_late():
        grad_cross, grad_cross_bf, cmixed, grad_cq, grad_ckv = cross_kept
        grads = jnp.concatenate(
            [
                mm_lt(first_bf, grad_cq).astype(BF),
                mm_lt(memory_low, grad_ckv).astype(BF),
                mm_lt(cmixed, grad_cross_bf).astype(BF),
            ],
            axis=1,
        )
        return grads, grad_cross + mm_rt(grad_cq, cross_full[:, :width])

    cross_grads, dec_first = lax.cond(
        is_enc,
        lambda: (jnp.zeros((width, 4 * width), BF), jnp.zeros((total, width), F32)),
        cross_late,
    )
    scored, q_grad_rows, grad_heat, query_grads, query_small_grads = queried

    def enc_back():
        grad_f, grad_h, grad_first, gain_two, shift_two = feed_back(
            memory_grad.astype(F32), enc_slope, enc_kept
        )
        return grad_f, grad_h, grad_first, (gain_two, shift_two)

    grad_f, grad_h, grad_first, norm_two = lax.cond(
        is_enc, enc_back, lambda: (dec_f, dec_h, dec_first, dec_norm)
    )

    grad_h, grad_f, grad_first, layer_rows = stage(grad_h, grad_f, grad_first, layer_rows)
    dec_home = links.home_dec(layer_rows)
    up_got = links.reduce_open(feed_in, grad_h)
    down_got = links.reduce_open(active, grad_f)
    cross_pair = cross_grads.reshape(2, width // 2, 4 * width)
    cross_got = links.flip(
        lax.dynamic_index_in_dim(cross_pair, 1 - core, 0, keepdims=False), "dec"
    )
    grad_one, gain_one, shift_one = norm_bwd(grad_first, kept_one, gains[0])
    grad_one_bf = grad_one.astype(BF)
    grad_mixed = mm_rt(grad_one_bf, w_out).astype(BF)
    up_got, down_got, cross_got, grad_mixed, dec_home = stage(
        up_got, down_got, cross_got, grad_mixed, dec_home
    )
    cross_sum = lax.dynamic_index_in_dim(cross_pair, core, 0, keepdims=False)
    cross_sum = (cross_sum.astype(F32) + cross_got.astype(F32)).astype(BF)
    cross_sum = cross_sum.reshape((2,) + (2,) * links.bits + (cross_rows, 4 * width))
    up_sum = links.reduce_own(feed_in, grad_h, up_got)
    down_sum = links.reduce_own(active, grad_f, down_got)

    def feed_steps(step):
        return [
            (up_sum, 1, step, "both", 0),
            (down_sum, 2, step, "both", 0),
            (cross_sum, 0, step, "dec", 1),
        ]

    up_sum, down_sum, cross_sum = links.reduce_steps(feed_steps(0))
    grad_joint = attend_back(
        joint, joint, joint, self_off, width, labels, causal, grad_mixed, True
    )
    up_sum, down_sum, cross_sum, grad_joint = stage(up_sum, down_sum, cross_sum, grad_joint)
    split_joint = [(0, joint_w // 2), (joint_w // 2, joint_w)]
    attn_jobs = [(stream_bf, grad_joint[:, a:b]) for a, b in split_joint]
    attn_jobs += [(mixed, grad_one_bf)]
    attn_got = [links.reduce_open(left, right) for left, right in attn_jobs]
    grad_rows = (grad_one + mm_rt(grad_joint, w_joint)).astype(BF)
    up_sum, down_sum, cross_sum = links.reduce_steps(feed_steps(1))

    def role_rows(vec):
        return vec.reshape(n, -1)

    def role_pair_rows(one, two):
        return jnp.stack([role_rows(one), role_rows(two)], axis=1).reshape(n, -1)

    def side_rows(vec):
        lead = vec.reshape(-1, vec.shape[-1]).shape[0]
        return vec.reshape(lead, 2 * n, -1).transpose(1, 0, 2).reshape(2 * n, -1)

    joint_cols = colsum(grad_joint)
    role_grads = jnp.concatenate(
        [
            role_rows(jnp.concatenate([joint_cols[:width], joint_cols[2 * width :]])),
            role_rows(colsum(grad_one_bf)),
            role_rows(colsum(grad_h)),
            role_rows(colsum(grad_f)),
            role_pair_rows(gain_one, norm_two[0]),
            role_pair_rows(shift_one, norm_two[1]),
        ],
        axis=-1,
    )
    def lead_rows(table):
        table = table.reshape(2, 2, half, -1).transpose(0, 2, 1, 3)
        return table.reshape(2, half, -1)

    cross_table = jnp.concatenate([side_rows(v) for v in cross_small_grads], axis=1)
    query_table = jnp.concatenate([side_rows(v) for v in query_small_grads], axis=1)
    small_grads = jnp.concatenate(
        [
            role_grads.reshape(2, half, n_role),
            lead_rows(cross_table),
            lead_rows(query_table),
            jnp.broadcast_to(grad_heat, (2, half, 1)),
        ],
        axis=2,
    )
    small_sum = lax.dynamic_index_in_dim(small_grads, core, 0, keepdims=False)
    small_got = links.flip(lax.dynamic_index_in_dim(small_grads, 1 - core, 0, keepdims=False))
    small_sum = (small_sum + small_got).reshape((2,) * links.bits + (1, -1))
    up_sum, down_sum, cross_sum, attn_got, grad_rows, small_sum = stage(
        up_sum, down_sum, cross_sum, attn_got, grad_rows, small_sum
    )
    rows_home = links.swap(grad_rows)
    for step in range(2, links.bits):
        up_sum = links.reduce_step(up_sum, 1, step)
        down_sum = links.reduce_step(down_sum, 2, step)
        cross_sum = links.reduce_step(cross_sum, 0, step, "dec", 1)
    attn_sum = [
        links.reduce_step(links.reduce_own(left, right, got), turn, 0)
        for turn, ((left, right), got) in enumerate(zip(attn_jobs, attn_got))
    ]
    small_sum = links.reduce_step(small_sum, 0, 0)
    per_block = inquiry_vectors.shape[1]
    score_row = jnp.pad(scored.reshape(1, -1), ((0, 0), (0, q_width - scored.size))).astype(BF)
    q_packet = jnp.concatenate([q_grad_rows.astype(BF), score_row])
    attn_sum, up_sum, down_sum, rows_home, small_sum, cross_sum, factors, q_packet = stage(
        attn_sum, up_sum, down_sum, rows_home, small_sum, cross_sum, factors, q_packet
    )
    up_own = links.swap(up_sum.reshape(-1, ff)).astype(F32)
    down_own = links.swap(down_sum.reshape(-1, width)).astype(F32)
    for step in range(1, links.bits):
        *attn_sum, small_sum = links.reduce_steps(
            [(v, turn, step, "both", 0) for turn, v in enumerate(attn_sum)]
            + [(small_sum, 0, step, "both", 0)]
        )
        if step + 1 < links.bits:
            attn_sum, small_sum, factors = stage(attn_sum, small_sum, factors)
    device = core * n + links.dp

    def own_columns(matrix, count):
        wide = matrix.shape[1]
        lines = lax.broadcasted_iota(jnp.int32, (wide, count), 0)
        places = lax.broadcasted_iota(jnp.int32, (wide, count), 1) + device * count
        return mm(matrix, (lines == places).astype(BF)).astype(BF)

    sizes, at, cols = [q_width] * 5 + [q_ff, q_ff] + [q_width] * 3, 0, []
    for size in sizes:
        cols.append(factors[0][:, at : at + size])
        at += size
    f_head, f_q, f_mixed, f_one, f_middle, f_hidden, f_active, f_two, f_asks, f_gmix = cols

    table = factors[1]
    all_asked, all_seen = factors[0].shape[0], table.shape[0]
    lines = lax.broadcasted_iota(jnp.int32, (all_seen, all_asked), 0) // QHEADS
    spread = (lines == lax.broadcasted_iota(jnp.int32, (all_seen, all_asked), 1)).astype(BF)
    row_head = lax.broadcasted_iota(jnp.int32, (all_seen, q_width), 0) % QHEADS
    col_head = lax.broadcasted_iota(jnp.int32, (all_seen, q_width), 1) // (q_width // QHEADS)

    def by_head(seen, other):
        wide = jnp.where(row_head == col_head, mm(spread, other), 0.0).astype(BF)
        return mm_lt(own_columns(seen, q_rows), wide)

    query_k_own = by_head(table[:, :q_width], f_asks) * (q_width // QHEADS) ** (-0.5)
    query_v_own = by_head(table[:, q_width:], f_gmix)
    query_q_own = mm_lt(own_columns(f_head, q_rows), f_q)
    query_out_own = mm_lt(own_columns(f_mixed, q_rows), f_one)
    query_up_own = mm_lt(own_columns(f_middle, q_rows), f_hidden)
    query_down_own = mm_lt(own_columns(f_active, q_rows * q_folds), f_two)
    query_own_mats = [
        jnp.concatenate([query_q_own, query_k_own, query_v_own], axis=1),
        query_out_own,
        query_up_own,
        query_down_own,
    ]
    attn_home = jnp.concatenate([v.reshape(-1, v.shape[-1]) for v in attn_sum], axis=1)
    attn_home = links.swap(attn_home).astype(F32)
    joint_own, out_own = attn_home[:, :joint_w], attn_home[:, joint_w:]
    cross_sum = cross_sum.reshape(2, cross_rows, 4 * width)
    cross_sum = jnp.where(is_enc, links.to_enc(cross_sum[0]), cross_sum[1]).astype(F32)
    cross_own_mats = [
        cross_sum[:, :width],
        cross_sum[:, width : 3 * width],
        cross_sum[:, 3 * width :],
    ]
    small_sum = small_sum.reshape(-1)
    role_own = links.swap(small_sum[:n_role])
    cross_pair = small_sum[n_role : n_role + 2 * n_cross].reshape(2, n_cross)
    query_pair = small_sum[n_role + 2 * n_cross : n_role + 2 * n_cross + 2 * n_query]
    pairs = jnp.concatenate([cross_pair, query_pair.reshape(2, n_query)], axis=1)
    keep_side = jnp.concatenate([jnp.where(is_enc, pairs[0], pairs[1]), small_sum[-1:]])
    send_side = jnp.concatenate([jnp.where(is_enc, pairs[1], pairs[0]), small_sum[-1:]])
    side_own = keep_side + links.across(send_side)
    cross_own = side_own[:n_cross]
    query_own = side_own[n_cross : n_cross + n_query]
    heat_total = side_own[-1:]

    layer_out = jnp.where(core == 0, enc_home, dec_home).reshape(1, micro, rows, width)
    input_grad = rows_home.astype(F32).reshape(1, micro, rows, width)

    q_home = links.home_enc(q_packet)
    q_mats = q_home[: micro * per_block].reshape(micro, per_block, q_width)
    s_mats = q_home[micro * per_block :, : scored.size].reshape(micro, 1, -1)
    second = jnp.concatenate(
        [q_mats[1], jnp.pad(s_mats[1], ((0, 0), (0, q_width - s_mats.shape[2])))]
    )
    got_second = lax.ppermute(second, "phase", [(0, 1)])
    question_grad = jnp.where(core == 0, q_mats[0], got_second[:per_block]).astype(F32)[None]
    own_scores = jnp.where(core == 0, s_mats[0], got_second[per_block:, : s_mats.shape[2]])
    scores = own_scores.astype(F32).reshape(1, asked, chosen_count)

    sizes = [
        intrinsic_probe_content_offset.shape[1],
        intrinsic_mixing_result_offset.shape[1],
        perceptron_widen_offset.shape[1],
        perceptron_narrow_offset.shape[1],
        2 * standardize_scales.shape[2],
        2 * standardize_shifts.shape[2],
    ]
    cut, role_out = 0, []
    for size in sizes:
        role_out.append(role_own[cut : cut + size])
        cut += size
    role_tuple = (
        joint_own[None],
        role_out[0][None],
        out_own[None],
        role_out[1][None],
        up_own[None],
        role_out[2][None],
        down_own[None],
        role_out[3][None],
        role_out[4].reshape(1, 2, -1),
        role_out[5].reshape(1, 2, -1),
    )
    c = cross_own.reshape(5, -1)
    cross_tuple = (
        cross_own_mats[0],
        c[0],
        cross_own_mats[1],
        c[1],
        cross_own_mats[2],
        c[2],
        c[3],
        c[4],
    )
    cut, q_out = 0, []
    for part in (
        retriever_probe_content_offset,
        retriever_mixing_result_offset,
        retriever_widen_offset,
        retriever_narrow_offset,
        retriever_standardize_scales,
        retriever_standardize_shifts,
    ):
        q_out.append(query_own[cut : cut + part.size].reshape(part.shape))
        cut += part.size
    query_tuple = (
        query_own_mats[0],
        q_out[0],
        query_own_mats[1],
        q_out[1],
        query_own_mats[2],
        q_out[2],
        query_own_mats[3],
        q_out[3],
        q_out[4],
        q_out[5],
    )
    return (
        (layer_out, input_grad, scores, question_grad, heat_total)
        + role_tuple
        + cross_tuple
        + query_tuple
    )


def solution(mesh):
    row = P(None, "dp", None)
    mat, vec = P("phase", "dp", None), P("phase", "dp")
    pair = P("phase", None, "dp")
    side_mat, side_vec = P(("phase", "dp"), None), P(("phase", "dp"))
    side_pair = P(None, ("phase", "dp"))
    role = (mat, vec, mat, vec, mat, vec, mat, vec, pair, pair)
    cross = (side_mat, side_vec, side_mat, side_vec, side_mat, side_vec, side_vec, side_vec)
    query = (side_mat, side_vec) * 4 + (side_pair, side_pair)
    stream = P("phase", None, "dp", None)
    in_specs = (stream,) + (row,) * 7 + (P(),) + role + cross + query
    out_specs = (stream, stream, mat, mat, P()) + role + cross + query
    return jax.shard_map(local, mesh=mesh, in_specs=in_specs, out_specs=out_specs, check_vma=False)
```
